32 devices in a mesh: fsdp: 4 (over z), ctx: 8 (over y, x, core).
Axes of the slice: x: 2, y: 2, z: 4, core: 2. Of those that a mesh axis runs over, the one named last changes fastest.
Arguments:
- query: bfloat16 [4, 2048, 4096], P('fsdp', 'ctx'), may hold values from -2.5 to 2.5
- key_value_rows: bfloat16 [4, 2048, 1024], P('fsdp', 'ctx'), may hold values from -2.5 to 2.5
- grad_out: bfloat16 [4, 2048, 4096], P('fsdp', 'ctx'), may hold values from -6 to 6
- doc_lengths: int32 [4, 8], P('fsdp'), may hold values from 1 to 512, 2048 in all within a row
- key_value_weight: bfloat16 [4096, 1024], P(('fsdp', 'ctx')), may hold values from -0.1875 to 0.1875
Outputs:
- grad_query: bfloat16 [4, 2048, 4096], P('fsdp', 'ctx')
- grad_kv: bfloat16 [4, 2048, 1024], P('fsdp', 'ctx')
- grad_input: bfloat16 [4, 2048, 4096], P('fsdp', 'ctx')
The draws below stay inside these ranges and needn't reach their ends.
Inputs may be any that keep to these rules, and one draw needn't show every extreme that they name: `doc_lengths`: each row sums to 2048; in each row the longest document has exactly 512 tokens.
All inputs are finite; a program needn't handle non-finite values.
Results may differ from the reference program's by a relative error of at most 0.0059.
Values may be sent and summed in bfloat16 or wider, within the bound.
A program may use at most 128 MiB of HBM per device.

```python
import math
import jax
import jax.numpy as jnp
import numpy as np
from jax import lax

QUERY_HEAD_COUNT = 32
KEY_VALUE_HEADS = 4
HEAD_SIZE = 128
INPUT_FEATURES = 4096
DOC_SHARDS = 2
TOK_DEV = 256
SEQUENCE_COUNT = 4
SEQUENCE_TOKENS = 2048
DOCS = 8
DOC_MAX = 512
N_CTX = 8


def steps_of(own_key, dims, shards, smallest, high):
    loudness, own = 1.0, jax.random.fold_in(own_key, 6)
    for position, parts in shards:
        heights = jnp.exp(jax.random.uniform(jax.random.fold_in(own, position), (parts,), jnp.float32, smallest / len(shards), high / len(shards)))
        loudness = loudness * jnp.repeat(heights, dims[position] // parts).reshape([-1 if axis == position else 1 for axis in range(len(dims))])
    return loudness


def split_up(count, total, bound, lean):
    weights = [(1 << 20) // math.isqrt(standing ** lean) + 1 for standing in range(2, count + 1)]
    rest, holding = total - bound - (count - 1), [1] * (count - 1)
    while rest > 0:
        free = [i for i in range(count - 1) if holding[i] < bound]
        whole, remaining = sum([weights[i] for i in free]), rest
        for i in free:
            extra = min(bound - holding[i], max(1, remaining * weights[i] // whole), rest)
            holding[i] = holding[i] + extra
            rest = rest - extra
    return np.array([bound] + holding)


def uneven_parts(rng, amount, total, reach, skew):
    if amount == 2:
        one = jax.random.randint(rng, (), max(1, total - reach), min(reach, total - 1) + 1)
        return jnp.stack([one, total - one])
    tallies = jnp.asarray(split_up(amount, total, reach, skew), jnp.int32)
    pairs = (amount - 1) // 2
    source_of, sink = tallies[1:1 + 2 * pairs:2], tallies[2:2 + 2 * pairs:2]
    slack = jnp.minimum(source_of - 1, reach - sink)
    moved = jax.random.randint(jax.random.fold_in(rng, 1), (pairs,), 0, 1 << 20) % (slack + 1)
    tallies = tallies.at[1:1 + 2 * pairs:2].set(source_of - moved).at[2:2 + 2 * pairs:2].set(sink + moved)
    return tallies[jax.random.permutation(jax.random.fold_in(rng, 2), amount)]


def centred(own_key, dims, deviation, limit, split=(), kind=jnp.bfloat16):
    result = jax.random.normal(own_key, dims, jnp.float32) * deviation
    if len(split) > 0:
        result = steps_of(own_key, dims, split, -0.22, 0.18) * result
    return jnp.clip(result, min=-limit, max=limit).astype(kind)


def setup_inputs(seed: int = 0) -> dict:
    streams_of = jax.random.split(jax.random.key(seed), 6)
    query = centred(streams_of[0], (SEQUENCE_COUNT, SEQUENCE_TOKENS, QUERY_HEAD_COUNT * HEAD_SIZE), 1.0, 2.5, ((0, 4), (1, 8)))
    key_value_rows = centred(streams_of[1], (SEQUENCE_COUNT, SEQUENCE_TOKENS, 2 * KEY_VALUE_HEADS * HEAD_SIZE), 1.0, 2.5, ((0, 4), (1, 8)))
    grad_out = centred(streams_of[2], (SEQUENCE_COUNT, SEQUENCE_TOKENS, QUERY_HEAD_COUNT * HEAD_SIZE), 1.0, 6.0, ((0, 4), (1, 8)))
    doc_lengths = jax.vmap(lambda own: uneven_parts(own, DOCS, SEQUENCE_TOKENS, DOC_MAX, 1))(jax.random.split(streams_of[3], SEQUENCE_COUNT)).reshape((SEQUENCE_COUNT, DOCS)).astype(jnp.int32)
    key_value_weight = centred(streams_of[4], (INPUT_FEATURES, 2 * KEY_VALUE_HEADS * HEAD_SIZE), (2 * KEY_VALUE_HEADS * HEAD_SIZE) ** -0.5, 0.1875, ((0, 32),))
    return dict(query=query, key_value_rows=key_value_rows, grad_out=grad_out, doc_lengths=doc_lengths, key_value_weight=key_value_weight)


def doc_number(positions, lengths):
    doc_ends = jnp.cumsum(lengths.astype(jnp.int32)).astype(jnp.int32)
    return jnp.sum((doc_ends[None, :] <= positions[:, None]).astype(jnp.int32), axis=1).astype(jnp.int32)


def build_mask(query_pos, key_pos, lengths):
    same_doc = doc_number(query_pos, lengths)[:, None] == doc_number(key_pos, lengths)[None, :]
    return same_doc & (key_pos[None, :] <= query_pos[:, None]) & (key_pos[None, :] >= 0)


def head_grads(query_cols, grad_cols, key_cols, value_cols, live):
    row_count = query_cols.shape[0]
    score_scale = HEAD_SIZE ** -0.5
    query_heads = query_cols.reshape(row_count, -1, HEAD_SIZE).astype(jnp.float32)
    grad_heads = grad_cols.reshape(row_count, -1, HEAD_SIZE).astype(jnp.float32)
    key_full = key_cols.astype(jnp.float32)
    value_full = value_cols.astype(jnp.float32)
    scores = jnp.einsum('rgd,wd->grw', query_heads, key_full) * score_scale
    exponent = jnp.where(live[None], jnp.exp(scores), jnp.zeros_like(scores))
    probabilities = exponent / jnp.sum(exponent, axis=2, keepdims=True)
    prob_low = lax.optimization_barrier(probabilities.astype(jnp.bfloat16)).astype(jnp.float32)
    attn_out = jnp.einsum('grw,wd->rgd', prob_low, value_full)
    row_delta = jnp.sum(grad_heads * attn_out, axis=2)
    prob_grad = jnp.einsum('rgd,wd->grw', grad_heads, value_full)
    score_grad = probabilities * (prob_grad - row_delta.T[:, :, None]) * score_scale
    score_low = lax.optimization_barrier(score_grad.astype(jnp.bfloat16)).astype(jnp.float32)
    query_grad = jnp.einsum('grw,wd->rgd', score_low, key_full).reshape(row_count, -1)
    key_grad = jnp.einsum('grw,rgd->wd', score_low, query_heads)
    value_grad = jnp.einsum('grw,rgd->wd', prob_low, grad_heads)
    return query_grad, key_grad, value_grad


def window_grads(query_rows, grad_rows, window, live):
    head_columns = QUERY_HEAD_COUNT // KEY_VALUE_HEADS * HEAD_SIZE
    key_value_columns = KEY_VALUE_HEADS * HEAD_SIZE
    query_list, key_list, value_list = [], [], []
    for current_head_index in range(KEY_VALUE_HEADS):
        query_grad, key_grad, value_grad = head_grads(
            query_rows[:, current_head_index * head_columns:(current_head_index + 1) * head_columns],
            grad_rows[:, current_head_index * head_columns:(current_head_index + 1) * head_columns],
            window[:, current_head_index * HEAD_SIZE:(current_head_index + 1) * HEAD_SIZE],
            window[:, key_value_columns + current_head_index * HEAD_SIZE:key_value_columns + (current_head_index + 1) * HEAD_SIZE],
            live)
        query_list.append(query_grad)
        key_list.append(key_grad)
        value_list.append(value_grad)
    return jnp.concatenate(query_list, axis=1), jnp.concatenate(key_list + value_list, axis=1)


def sequence_grads(query, key_value_rows, grad_out, lengths):
    seq_len = query.shape[0]
    row_count = TOK_DEV
    lead_rows = DOC_SHARDS * TOK_DEV
    padded = jnp.concatenate([jnp.zeros((lead_rows, key_value_rows.shape[1]), key_value_rows.dtype), key_value_rows], axis=0)

    def block_step(window_acc, block_index):
        first_row = (block_index * row_count).astype(jnp.int32)
        query_rows = lax.dynamic_slice_in_dim(query, first_row, row_count, 0)
        grad_rows = lax.dynamic_slice_in_dim(grad_out, first_row, row_count, 0)
        window = lax.dynamic_slice_in_dim(padded, first_row, lead_rows + row_count, 0)
        query_pos = first_row + jnp.arange(row_count, dtype=jnp.int32)
        key_pos = first_row - lead_rows + jnp.arange(lead_rows + row_count, dtype=jnp.int32)
        live = build_mask(query_pos, key_pos, lengths)
        query_grad, window_grad = window_grads(query_rows, grad_rows, window, live)
        previous = lax.dynamic_slice_in_dim(window_acc, first_row, lead_rows + row_count, 0)
        window_acc = lax.dynamic_update_slice_in_dim(window_acc, previous + window_grad, first_row, 0)
        return window_acc, query_grad.astype(jnp.bfloat16)

    starting_state = jnp.zeros((seq_len + lead_rows, key_value_rows.shape[1]), jnp.float32)
    window_acc, query_blocks = lax.scan(block_step, starting_state, jnp.arange(N_CTX, dtype=jnp.int32))
    grad_kv = window_acc[lead_rows:].astype(jnp.bfloat16)
    return query_blocks.reshape(seq_len, -1), grad_kv


def reference(query, key_value_rows, grad_out, doc_lengths, key_value_weight):
    query_list, kv_list, input_list = [], [], []
    for sequence in range(SEQUENCE_COUNT):
        query_grad, grad_kv = sequence_grads(query[sequence], key_value_rows[sequence], grad_out[sequence], doc_lengths[sequence])
        grad_input = jnp.dot(grad_kv, key_value_weight.T, preferred_element_type=jnp.float32).astype(jnp.bfloat16)
        query_list.append(query_grad)
        kv_list.append(grad_kv)
        input_list.append(grad_input)
    return jnp.stack(query_list), jnp.stack(kv_list), jnp.stack(input_list)
```

```python
import functools

import jax
import jax.numpy as jnp
from jax import lax
from jax.experimental import pallas as pl
from jax.experimental.pallas import tpu as pltpu
from jax.sharding import PartitionSpec as P

QUERY_HEAD_COUNT = 32
KEY_VALUE_HEADS = 4
HEAD_SIZE = 128
DOC_SHARDS = 2
GROUP = QUERY_HEAD_COUNT // KEY_VALUE_HEADS
LOG2E = 1.4426950408889634


def dot(a, b, dims):
    return lax.dot_general(a, b, (dims, ((), ())), preferred_element_type=jnp.float32)


def gradients_kernel(
    shape, lengths, query_hbm, grad_hbm, kv_hbm, w_own, grad_query, grad_kv, w_all,
    query, grad, kv0, in_sem, kv_sem,
    window, staged, landed, own, bias, dk, dv,
    kv_send, kv_recv, g_send, g_recv, z_send, r_send, l_send, p_send, w_recv, p_recv, local_sem,
):
    shards, count = shape
    chips = count // 2
    half = chips // 2
    width = int(chips ** 0.5)
    rows = query.shape[0]
    group_width = GROUP * HEAD_SIZE
    w_rows = w_own.shape[0]
    keys = (DOC_SHARDS + 1) * rows
    scale = HEAD_SIZE ** (-0.5)
    z = lax.axis_index("fsdp")
    me = lax.axis_index("ctx")
    core = lax.rem(me, 2)
    chip = me // 2
    line = chip // width
    column = lax.rem(chip, width)
    odd = lax.rem(line, 2)
    place = line * width + column + odd * (width - 1 - 2 * column)

    def ring_ctx(spot):
        spot = lax.rem(spot + chips, chips)
        row = spot // width
        col = lax.rem(spot, width)
        return 2 * (row * width + col + lax.rem(row, 2) * (width - 1 - 2 * col)) + core

    right = ring_ctx(place + 1)
    left = ring_ctx(place - 1)
    partner = me + 1 - 2 * core

    def query_in(g):
        cols = pl.ds(pl.multiple_of(g * group_width, HEAD_SIZE), group_width)
        return pltpu.make_async_copy(query_hbm.at[:, cols], query.at[:, cols], in_sem.at[0, g])

    def grad_in(g):
        cols = pl.ds(pl.multiple_of(g * group_width, HEAD_SIZE), group_width)
        return pltpu.make_async_copy(grad_hbm.at[:, cols], grad.at[:, cols], in_sem.at[1, g])

    kv_in = pltpu.make_async_copy(kv_hbm, kv0, kv_sem)
    kv_in.start()
    for g in range(KEY_VALUE_HEADS):
        query_in(g).start()
        grad_in(g).start()

    barrier = pltpu.get_barrier_semaphore()
    peers = [(z, lax.rem(me + o + count, count)) for o in (1, 2, -1, -2)]
    peers += [(lax.rem(z + r, shards), me) for r in range(1, shards)]
    peers += [(z, right), (z, left), (z, partner)]
    for peer in peers:
        pl.semaphore_signal(barrier, inc=1, device_id=peer, device_id_type=pl.DeviceIdType.MESH)
    pl.semaphore_wait(barrier, len(peers))

    def remote(src, dst, send, recv, device):
        return pltpu.make_async_remote_copy(
            src_ref=src, dst_ref=dst, send_sem=send, recv_sem=recv,
            device_id=device, device_id_type=pl.DeviceIdType.MESH,
        )

    def kv_copy(o, g, part):
        cols = pl.ds(pl.multiple_of((part * KEY_VALUE_HEADS + g) * HEAD_SIZE, HEAD_SIZE), HEAD_SIZE)
        return remote(
            kv_hbm.at[:, cols], window.at[o, :, cols], kv_send.at[o, g, part], kv_recv.at[o, g, part],
            (z, lax.rem(me + o + 1, count)),
        )

    def kv_relay(g, part):
        cols = pl.ds(pl.multiple_of((part * KEY_VALUE_HEADS + g) * HEAD_SIZE, HEAD_SIZE), HEAD_SIZE)
        return remote(
            window.at[1, :, cols], window.at[0, :, cols], kv_send.at[0, g, part], kv_recv.at[0, g, part],
            (z, partner),
        )

    sends_kv = [core == 0, me + 2 < count]
    relays_kv = (core == 1) & (me >= 2)

    def grad_copy(o, g):
        return remote(
            staged.at[o, g], landed.at[o, g], g_send.at[o, g], g_recv.at[o, g],
            (z, lax.rem(me - o - 1 + count, count)),
        )

    def block(zz, spot, flip=False):
        at = ring_ctx(spot)
        if flip:
            at = at + 1 - 2 * core
        return w_all.at[pl.ds(pl.multiple_of((zz * count + at) * w_rows, w_rows), w_rows)]

    def w_copy(zz, spot, sems, arrive, device, mine=False):
        spot = lax.rem(spot + chips, chips)
        src = w_own if mine else block(zz, spot)
        return remote(src, block(zz, spot), sems.at[zz, spot], arrive.at[zz, spot], device)

    def shard(r):
        return lax.rem(z - r + shards, shards)

    def w_arrived(r, t):
        w_copy(shard(r), place + t, r_send, w_recv, (z, right)).wait_recv()

    def takes_right(spot, zz):
        at = lax.rem(lax.rem(spot + chips, chips), 4)
        turn = lax.rem(zz, 4)
        even = lax.rem(at, 2) == 0
        return even | ((at == 1) & (turn >= 1)) | ((at == 3) & (turn >= 2))

    def each_copy(r, t, act):
        zz = shard(r)
        mine = r == 0 and t == 0
        if t == 0:
            act(w_copy(zz, place, r_send, w_recv, (z, right), mine))
            act(w_copy(zz, place, l_send, w_recv, (z, left), mine))
        elif -half + 1 <= t < 0:
            copy = w_copy(zz, place + t, r_send, w_recv, (z, right))
            if t > -half + 1:
                act(copy)
            else:
                pl.when(takes_right(place + 1, zz))(lambda: act(copy))
        elif 0 < t <= half - 1:
            copy = w_copy(zz, place + t, l_send, w_recv, (z, left))
            if t < half - 1:
                act(copy)
            else:
                pl.when(jnp.logical_not(takes_right(place - 1, zz)))(lambda: act(copy))
        act(w_copy(zz, place + t, p_send, p_recv, (z, partner), mine))

    def z_copy(r):
        to = lax.rem(z + r, shards)
        return remote(w_own, block(z, place), z_send.at[to], w_recv.at[z, place], (to, me))

    for g in range(KEY_VALUE_HEADS):
        for o in range(DOC_SHARDS):
            @pl.when(sends_kv[o])
            def _():
                kv_copy(o, g, 0).start()
                kv_copy(o, g, 1).start()

    for r in range(1, shards):
        z_copy(r).start()
    each_copy(0, 0, lambda c: c.start())
    local = pltpu.make_async_copy(w_own, block(z, place), local_sem)
    local.start()

    for o in range(DOC_SHARDS):
        @pl.when(me < o + 1)
        def _():
            window[o] = jnp.zeros(window.shape[1:], window.dtype)

        @pl.when(me + o + 1 >= count)
        def _():
            landed[o] = jnp.zeros(landed.shape[1:], landed.dtype)

    first = me * rows
    pos = first + lax.broadcasted_iota(jnp.int32, (1, rows), 1)
    start = jnp.zeros((1, rows), jnp.int32)
    end = jnp.int32(0)
    for d in range(lengths.shape[1]):
        end = end + lengths[0, d]
        start = jnp.where(pos >= end, end, start)
    key_pos = first - DOC_SHARDS * rows + lax.broadcasted_iota(jnp.int32, (keys, rows), 0)
    live = (key_pos >= start) & (key_pos <= pos)
    bias[...] = jnp.where(live, 0.0, -1e30)

    def group(g, carry):
        for o in reversed(range(DOC_SHARDS)):
            @pl.when(me >= o + 1)
            def _():
                kv_copy(o, g, 0).wait_recv()
                kv_copy(o, g, 1).wait_recv()

            if o == 1:
                @pl.when(relays_kv)
                def _():
                    kv_relay(g, 0).start()
                    kv_relay(g, 1).start()
        query_in(g).wait()
        grad_in(g).wait()

        @pl.when(g == 0)
        def _():
            kv_in.wait()
        kc = pl.ds(pl.multiple_of(g * HEAD_SIZE, HEAD_SIZE), HEAD_SIZE)
        vc = pl.ds(pl.multiple_of((g + KEY_VALUE_HEADS) * HEAD_SIZE, HEAD_SIZE), HEAD_SIZE)
        key = jnp.concatenate([window[1, :, kc], window[0, :, kc], kv0[:, kc]], axis=0)
        value = jnp.concatenate([window[1, :, vc], window[0, :, vc], kv0[:, vc]], axis=0)
        dk[...] = jnp.zeros_like(dk)
        dv[...] = jnp.zeros_like(dv)
        for h in range(GROUP):
            cols = pl.ds(pl.multiple_of((g * GROUP + h) * HEAD_SIZE, HEAD_SIZE), HEAD_SIZE)
            q = query[:, cols]
            go = grad[:, cols]
            s = dot(key, q, ((1,), (1,)))
            e = jnp.exp2(s * (scale * LOG2E) + bias[...])
            dp = dot(value, go, ((1,), (1,)))
            inv = 1.0 / jnp.sum(e, axis=0, keepdims=True)
            delta = jnp.sum(e * dp, axis=0, keepdims=True) * inv
            p = e * inv
            ds = (p * (dp - delta)).astype(jnp.bfloat16)
            dv[...] += dot(p.astype(jnp.bfloat16), go, ((1,), (0,)))
            dk[...] += dot(ds, q, ((1,), (0,)))
            dq = dot(key, ds, ((0,), (0,)))
            grad_query[:, cols] = (dq * scale).T.astype(jnp.bfloat16)
        for o in range(DOC_SHARDS):
            part = slice((DOC_SHARDS - 1 - o) * rows, (DOC_SHARDS - o) * rows)
            staged[o, g, 0] = (dk[part, :] * scale).astype(jnp.bfloat16)
            staged[o, g, 1] = dv[part, :].astype(jnp.bfloat16)
        own[g, 0] = dk[DOC_SHARDS * rows:, :] * scale
        own[g, 1] = dv[DOC_SHARDS * rows:, :]
        for o in range(DOC_SHARDS):
            @pl.when(me >= o + 1)
            def _():
                grad_copy(o, g).start()
        for k in range(KEY_VALUE_HEADS):
            turn = [r for r in range(1, shards) if min(r - 1, KEY_VALUE_HEADS - 1) == k]
            if turn:
                @pl.when(g == k)
                def _():
                    for r in turn:
                        w_arrived(r, 0)
                        each_copy(r, 0, lambda c: c.start())
        return carry

    lax.fori_loop(0, KEY_VALUE_HEADS, group, 0)

    for t in range(1, half):
        for r in range(shards):
            for side in (-t, t):
                w_arrived(r, side)
                each_copy(r, side, lambda c: c.start())

    for g in range(KEY_VALUE_HEADS):
        for o in range(DOC_SHARDS):
            @pl.when(me + o + 1 < count)
            def _():
                grad_copy(o, g).wait_recv()
        for part in range(2):
            total = own[g, part]
            for o in range(DOC_SHARDS):
                total = total + landed[o, g, part].astype(jnp.float32)
            at = (part * KEY_VALUE_HEADS + g) * HEAD_SIZE
            grad_kv[:, at:at + HEAD_SIZE] = total.astype(jnp.bfloat16)

    for r in range(shards):
        w_arrived(r, half)
        each_copy(r, half, lambda c: c.start())

    for r in range(shards):
        for t in range(-half + 1, half + 1):
            w_copy(shard(r), place + t, p_send, p_recv, (z, partner)).wait_recv()
            each_copy(r, t, lambda c: c.wait_send())
    for r in range(1, shards):
        z_copy(r).wait_send()
    local.wait()
    for g in range(KEY_VALUE_HEADS):
        @pl.when(relays_kv)
        def _():
            kv_relay(g, 0).wait_send()
            kv_relay(g, 1).wait_send()

        for o in range(DOC_SHARDS):
            @pl.when(sends_kv[o])
            def _():
                kv_copy(o, g, 0).wait_send()
                kv_copy(o, g, 1).wait_send()

            @pl.when(me >= o + 1)
            def _():
                grad_copy(o, g).wait_send()


def gradients(shape, lengths, query, grad, kv0, w_own):
    rows, width = query.shape
    keys = (DOC_SHARDS + 1) * rows
    w_rows, columns = w_own.shape
    shards, count = shape
    chips = count // 2
    vmem = pl.BlockSpec(memory_space=pltpu.VMEM)
    dma = pltpu.SemaphoreType.DMA
    parts = (DOC_SHARDS, KEY_VALUE_HEADS, 2, rows, HEAD_SIZE)
    return pl.pallas_call(
        functools.partial(gradients_kernel, shape),
        in_specs=[pl.BlockSpec(memory_space=pltpu.SMEM)] + [pl.BlockSpec(memory_space=pltpu.HBM)] * 4,
        out_specs=[pl.BlockSpec(memory_space=pltpu.VMEM)]*3,
        out_shape=[
            pltpu.VMEM((rows, width), jnp.bfloat16),
            pltpu.VMEM((rows, columns), jnp.bfloat16),
            pltpu.VMEM((w_rows * shards * count, columns), jnp.bfloat16),
        ],
        scratch_shapes=[
            pltpu.VMEM((rows, width), jnp.bfloat16),
            pltpu.VMEM((rows, width), jnp.bfloat16),
            pltpu.VMEM((rows, columns), jnp.bfloat16),
            dma((2, KEY_VALUE_HEADS)),
            dma,
            pltpu.VMEM((DOC_SHARDS, rows, columns), jnp.bfloat16),
            pltpu.VMEM(parts, jnp.bfloat16),
            pltpu.VMEM(parts, jnp.bfloat16),
            pltpu.VMEM(parts[1:], jnp.float32),
            pltpu.VMEM((keys, rows), jnp.float32),
            pltpu.VMEM((keys, HEAD_SIZE), jnp.float32),
            pltpu.VMEM((keys, HEAD_SIZE), jnp.float32),
            dma((DOC_SHARDS, KEY_VALUE_HEADS, 2)),
            dma((DOC_SHARDS, KEY_VALUE_HEADS, 2)),
            dma((DOC_SHARDS, KEY_VALUE_HEADS)),
            dma((DOC_SHARDS, KEY_VALUE_HEADS)),
            dma((shards,)),
            dma((shards, chips)),
            dma((shards, chips)),
            dma((shards, chips)),
            dma((shards, chips)),
            dma((shards, chips)),
            dma,
        ],
        compiler_params=pltpu.CompilerParams(
            vmem_limit_bytes=53*1024*1024, collective_id=0, has_side_effects=True
        ),
    )(lengths, query, grad, kv0, w_own)


def finish_kernel(q_ref, kv_ref, w_ref, q_out, kv_out, in_out, buf, sems):
    chunks = sems.shape[0] - 2
    step = buf.shape[1] // chunks
    qc = pltpu.make_async_copy(q_ref, q_out, sems.at[chunks])
    kc = pltpu.make_async_copy(kv_ref, kv_out, sems.at[chunks + 1])
    qc.start()
    kc.start()
    def cp(n):
        cols = pl.ds(n * step, step)
        return pltpu.make_async_copy(buf.at[:, cols], in_out.at[:, cols], sems.at[n])
    for n in range(chunks):
        buf[:, n * step:(n + 1) * step] = dot(kv_ref[...], w_ref[n * step:(n + 1) * step, :], ((1,), (1,))).astype(jnp.bfloat16)
        cp(n).start()
    for n in range(chunks):
        cp(n).wait()
    qc.wait()
    kc.wait()


def finish(grad_query, grad_kv, weight):
    rows, width = grad_query.shape
    feats = weight.shape[0]
    anyspec = pl.BlockSpec(memory_space=pl.ANY)
    vm = pl.BlockSpec(memory_space=pltpu.VMEM)
    return pl.pallas_call(
        finish_kernel,
        in_specs=[vm, vm, vm],
        out_specs=[anyspec] * 3,
        out_shape=[
            jax.ShapeDtypeStruct((rows, width), jnp.bfloat16),
            jax.ShapeDtypeStruct(grad_kv.shape, jnp.bfloat16),
            jax.ShapeDtypeStruct((rows, feats), jnp.bfloat16),
        ],
        scratch_shapes=[pltpu.VMEM((rows, feats), jnp.bfloat16), pltpu.SemaphoreType.DMA((10,))],
        compiler_params=pltpu.CompilerParams(vmem_limit_bytes=20*1024*1024),
    )(grad_query, grad_kv, weight)


def body(query, key_value_rows, grad_out, doc_lengths, key_value_weight):
    shape = (lax.axis_size("fsdp"), lax.axis_size("ctx"))
    grad_query, grad_kv, weight = gradients(
        shape, doc_lengths, query[0], grad_out[0], key_value_rows[0], key_value_weight
    )
    grad_query, grad_kv, grad_input = finish(grad_query, grad_kv, weight)
    return (grad_query[None], grad_kv[None], grad_input[None])


def solution(mesh):
    in_specs = (
        P("fsdp", "ctx", None),
        P("fsdp", "ctx", None),
        P("fsdp", "ctx", None),
        P("fsdp", None),
        P(("fsdp", "ctx"), None),
    )
    out_specs = (P("fsdp", "ctx", None), P("fsdp", "ctx", None), P("fsdp", "ctx", None))
    return jax.shard_map(body, mesh=mesh, in_specs=in_specs, out_specs=out_specs, check_vma=False)
```

```python
import functools

import jax
import jax.numpy as jnp
from jax import lax
from jax.experimental import pallas as pl
from jax.experimental.pallas import tpu as pltpu
from jax.sharding import PartitionSpec as P

QUERY_HEAD_COUNT = 32
KEY_VALUE_HEADS = 4
HEAD_SIZE = 128
DOC_SHARDS = 2
GROUP = QUERY_HEAD_COUNT // KEY_VALUE_HEADS
STEP = 2
LOG2E = 1.4426950408889634


def dot(a, b, dims):
    return lax.dot_general(a, b, (dims, ((), ())), preferred_element_type=jnp.float32)


def gradients_kernel(
    shape, lengths, query_hbm, grad_hbm, kv_hbm, w_own, grad_query, grad_kv, w_all,
    query, grad, kv0, in_sem, kv_sem,
    window, staged, landed, own, bias, dk, dv,
    kv_send, kv_recv, g_send, g_recv, z_send, r_send, l_send, p_send, w_recv, p_recv, local_sem,
):
    shards, count = shape
    chips = count // 2
    half = chips // 2
    width = int(chips ** 0.5)
    rows = query.shape[0]
    group_width = GROUP * HEAD_SIZE
    w_rows = w_own.shape[0]
    keys = (DOC_SHARDS + 1) * rows
    scale = HEAD_SIZE ** (-0.5)
    z = lax.axis_index("fsdp")
    me = lax.axis_index("ctx")
    core = lax.rem(me, 2)
    chip = me // 2
    line = chip // width
    column = lax.rem(chip, width)
    odd = lax.rem(line, 2)
    place = line * width + column + odd * (width - 1 - 2 * column)

    def ring_ctx(spot):
        spot = lax.rem(spot + chips, chips)
        row = spot // width
        col = lax.rem(spot, width)
        return 2 * (row * width + col + lax.rem(row, 2) * (width - 1 - 2 * col)) + core

    right = ring_ctx(place + 1)
    left = ring_ctx(place - 1)
    partner = me + 1 - 2 * core

    def query_in(g):
        cols = pl.ds(pl.multiple_of(g * group_width, HEAD_SIZE), group_width)
        return pltpu.make_async_copy(query_hbm.at[:, cols], query.at[:, cols], in_sem.at[0, g])

    def grad_in(g):
        cols = pl.ds(pl.multiple_of(g * group_width, HEAD_SIZE), group_width)
        return pltpu.make_async_copy(grad_hbm.at[:, cols], grad.at[:, cols], in_sem.at[1, g])

    kv_in = pltpu.make_async_copy(kv_hbm, kv0, kv_sem)
    kv_in.start()
    for g in range(KEY_VALUE_HEADS):
        query_in(g).start()
        grad_in(g).start()

    barrier = pltpu.get_barrier_semaphore()
    peers = [(z, lax.rem(me + o + count, count)) for o in (1, 2, -1, -2)]
    peers += [(lax.rem(z + r, shards), me) for r in range(1, shards)]
    peers += [(z, right), (z, left), (z, partner)]
    for peer in peers:
        pl.semaphore_signal(barrier, inc=1, device_id=peer, device_id_type=pl.DeviceIdType.MESH)
    pl.semaphore_wait(barrier, len(peers))

    def remote(src, dst, send, recv, device):
        return pltpu.make_async_remote_copy(
            src_ref=src, dst_ref=dst, send_sem=send, recv_sem=recv,
            device_id=device, device_id_type=pl.DeviceIdType.MESH,
        )

    def kv_copy(o, g, part):
        cols = pl.ds(pl.multiple_of((part * KEY_VALUE_HEADS + g) * HEAD_SIZE, HEAD_SIZE), HEAD_SIZE)
        return remote(
            kv_hbm.at[:, cols], window.at[o, :, cols], kv_send.at[o, g, part], kv_recv.at[o, g, part],
            (z, lax.rem(me + o + 1, count)),
        )

    def kv_relay(g, part):
        cols = pl.ds(pl.multiple_of((part * KEY_VALUE_HEADS + g) * HEAD_SIZE, HEAD_SIZE), HEAD_SIZE)
        return remote(
            window.at[1, :, cols], window.at[0, :, cols], kv_send.at[0, g, part], kv_recv.at[0, g, part],
            (z, partner),
        )

    sends_kv = [core == 0, me + 2 < count]
    relays_kv = (core == 1) & (me >= 2)

    def grad_copy(o, g):
        return remote(
            staged.at[o, g], landed.at[o, g], g_send.at[o, g], g_recv.at[o, g],
            (z, lax.rem(me - o - 1 + count, count)),
        )

    def block(zz, spot, flip=False):
        at = ring_ctx(spot)
        if flip:
            at = at + 1 - 2 * core
        return w_all.at[pl.ds(pl.multiple_of((zz * count + at) * w_rows, w_rows), w_rows)]

    def w_copy(zz, spot, sems, arrive, device, mine=False):
        spot = lax.rem(spot + chips, chips)
        src = w_own if mine else block(zz, spot)
        return remote(src, block(zz, spot), sems.at[zz, spot], arrive.at[zz, spot], device)

    def shard(r):
        return lax.rem(z - r + shards, shards)

    def w_arrived(r, t):
        w_copy(shard(r), place + t, r_send, w_recv, (z, right)).wait_recv()

    def takes_right(spot, zz):
        at = lax.rem(lax.rem(spot + chips, chips), 4)
        turn = lax.rem(zz, 4)
        even = lax.rem(at, 2) == 0
        return even | ((at == 1) & (turn >= 1)) | ((at == 3) & (turn >= 2))

    def each_copy(r, t, act):
        zz = shard(r)
        mine = r == 0 and t == 0
        if t == 0:
            act(w_copy(zz, place, r_send, w_recv, (z, right), mine))
            act(w_copy(zz, place, l_send, w_recv, (z, left), mine))
        elif -half + 1 <= t < 0:
            copy = w_copy(zz, place + t, r_send, w_recv, (z, right))
            if t > -half + 1:
                act(copy)
            else:
                pl.when(takes_right(place + 1, zz))(lambda: act(copy))
        elif 0 < t <= half - 1:
            copy = w_copy(zz, place + t, l_send, w_recv, (z, left))
            if t < half - 1:
                act(copy)
            else:
                pl.when(jnp.logical_not(takes_right(place - 1, zz)))(lambda: act(copy))
        act(w_copy(zz, place + t, p_send, p_recv, (z, partner), mine))

    def z_copy(r):
        to = lax.rem(z + r, shards)
        return remote(w_own, block(z, place), z_send.at[to], w_recv.at[z, place], (to, me))

    for g in range(KEY_VALUE_HEADS):
        for o in range(DOC_SHARDS):
            @pl.when(sends_kv[o])
            def _():
                kv_copy(o, g, 0).start()
                kv_copy(o, g, 1).start()

    for r in range(1, shards):
        z_copy(r).start()
    each_copy(0, 0, lambda c: c.start())
    local = pltpu.make_async_copy(w_own, block(z, place), local_sem)
    local.start()

    for o in range(DOC_SHARDS):
        @pl.when(me < o + 1)
        def _():
            window[o] = jnp.zeros(window.shape[1:], window.dtype)

        @pl.when(me + o + 1 >= count)
        def _():
            landed[o] = jnp.zeros(landed.shape[1:], landed.dtype)

    first = me * rows
    pos = first + lax.broadcasted_iota(jnp.int32, (1, rows), 1)
    start = jnp.zeros((1, rows), jnp.int32)
    end = jnp.int32(0)
    for d in range(lengths.shape[1]):
        end = end + lengths[0, d]
        start = jnp.where(pos >= end, end, start)
    key_pos = first - DOC_SHARDS * rows + lax.broadcasted_iota(jnp.int32, (keys, rows), 0)
    live = (key_pos >= start) & (key_pos <= pos)
    bias[...] = jnp.where(live, 0.0, -1e30)

    def group(g, carry):
        for o in reversed(range(DOC_SHARDS)):
            @pl.when(me >= o + 1)
            def _():
                kv_copy(o, g, 0).wait_recv()
                kv_copy(o, g, 1).wait_recv()

            if o == 1:
                @pl.when(relays_kv)
                def _():
                    kv_relay(g, 0).start()
                    kv_relay(g, 1).start()
        query_in(g).wait()
        grad_in(g).wait()

        @pl.when(g == 0)
        def _():
            kv_in.wait()
        kc = pl.ds(pl.multiple_of(g * HEAD_SIZE, HEAD_SIZE), HEAD_SIZE)
        vc = pl.ds(pl.multiple_of((g + KEY_VALUE_HEADS) * HEAD_SIZE, HEAD_SIZE), HEAD_SIZE)
        key = jnp.concatenate([window[1, :, kc], window[0, :, kc], kv0[:, kc]], axis=0)
        value = jnp.concatenate([window[1, :, vc], window[0, :, vc], kv0[:, vc]], axis=0)
        dk[...] = jnp.zeros_like(dk)
        dv[...] = jnp.zeros_like(dv)
        for h in range(GROUP):
            cols = pl.ds(pl.multiple_of((g * GROUP + h) * HEAD_SIZE, HEAD_SIZE), HEAD_SIZE)
            q = query[:, cols]
            go = grad[:, cols]
            s = dot(key, q, ((1,), (1,)))
            e = jnp.exp2(s * (scale * LOG2E) + bias[...])
            dp = dot(value, go, ((1,), (1,)))
            inv = 1.0 / jnp.sum(e, axis=0, keepdims=True)
            delta = jnp.sum(e * dp, axis=0, keepdims=True) * inv
            p = e * inv
            ds = (p * (dp - delta)).astype(jnp.bfloat16)
            dv[...] += dot(p.astype(jnp.bfloat16), go, ((1,), (0,)))
            dk[...] += dot(ds, q, ((1,), (0,)))
            dq = dot(key, ds, ((0,), (0,)))
            grad_query[:, cols] = (dq * scale).T.astype(jnp.bfloat16)
        for o in range(DOC_SHARDS):
            part = slice((DOC_SHARDS - 1 - o) * rows, (DOC_SHARDS - o) * rows)
            staged[o, g, 0] = (dk[part, :] * scale).astype(jnp.bfloat16)
            staged[o, g, 1] = dv[part, :].astype(jnp.bfloat16)
        own[g, 0] = dk[DOC_SHARDS * rows:, :] * scale
        own[g, 1] = dv[DOC_SHARDS * rows:, :]
        for o in range(DOC_SHARDS):
            @pl.when(me >= o + 1)
            def _():
                grad_copy(o, g).start()
        for k in range(KEY_VALUE_HEADS):
            turn = [r for r in range(1, shards) if min(r - 1, KEY_VALUE_HEADS - 1) == k]
            if turn:
                @pl.when(g == k)
                def _():
                    for r in turn:
                        w_arrived(r, 0)
                        each_copy(r, 0, lambda c: c.start())
        return carry

    lax.fori_loop(0, KEY_VALUE_HEADS, group, 0)

    for t in range(1, half):
        for r in range(shards):
            for side in (-t, t):
                w_arrived(r, side)
                each_copy(r, side, lambda c: c.start())

    for g in range(KEY_VALUE_HEADS):
        for o in range(DOC_SHARDS):
            @pl.when(me + o + 1 < count)
            def _():
                grad_copy(o, g).wait_recv()
        for part in range(2):
            total = own[g, part]
            for o in range(DOC_SHARDS):
                total = total + landed[o, g, part].astype(jnp.float32)
            at = (part * KEY_VALUE_HEADS + g) * HEAD_SIZE
            grad_kv[:, at:at + HEAD_SIZE] = total.astype(jnp.bfloat16)

    for r in range(shards):
        w_arrived(r, half)
        each_copy(r, half, lambda c: c.start())

    for r in range(shards):
        for t in range(-half + 1, half + 1):
            w_copy(shard(r), place + t, p_send, p_recv, (z, partner)).wait_recv()
            each_copy(r, t, lambda c: c.wait_send())
    for r in range(1, shards):
        z_copy(r).wait_send()
    local.wait()
    for g in range(KEY_VALUE_HEADS):
        @pl.when(relays_kv)
        def _():
            kv_relay(g, 0).wait_send()
            kv_relay(g, 1).wait_send()

        for o in range(DOC_SHARDS):
            @pl.when(sends_kv[o])
            def _():
                kv_copy(o, g, 0).wait_send()
                kv_copy(o, g, 1).wait_send()

            @pl.when(me >= o + 1)
            def _():
                grad_copy(o, g).wait_send()


def gradients(shape, lengths, query, grad, kv0, w_own):
    rows, width = query.shape
    keys = (DOC_SHARDS + 1) * rows
    w_rows, columns = w_own.shape
    shards, count = shape
    chips = count // 2
    vmem = pl.BlockSpec(memory_space=pltpu.VMEM)
    dma = pltpu.SemaphoreType.DMA
    parts = (DOC_SHARDS, KEY_VALUE_HEADS, 2, rows, HEAD_SIZE)
    return pl.pallas_call(
        functools.partial(gradients_kernel, shape),
        in_specs=[pl.BlockSpec(memory_space=pltpu.SMEM)] + [pl.BlockSpec(memory_space=pltpu.HBM)] * 4,
        out_specs=[pl.BlockSpec(memory_space=pltpu.VMEM)]*3,
        out_shape=[
            pltpu.VMEM((rows, width), jnp.bfloat16),
            pltpu.VMEM((rows, columns), jnp.bfloat16),
            pltpu.VMEM((w_rows * shards * count, columns), jnp.bfloat16),
        ],
        scratch_shapes=[
            pltpu.VMEM((rows, width), jnp.bfloat16),
            pltpu.VMEM((rows, width), jnp.bfloat16),
            pltpu.VMEM((rows, columns), jnp.bfloat16),
            dma((2, KEY_VALUE_HEADS)),
            dma,
            pltpu.VMEM((DOC_SHARDS, rows, columns), jnp.bfloat16),
            pltpu.VMEM(parts, jnp.bfloat16),
            pltpu.VMEM(parts, jnp.bfloat16),
            pltpu.VMEM(parts[1:], jnp.float32),
            pltpu.VMEM((keys, rows), jnp.float32),
            pltpu.VMEM((keys, HEAD_SIZE), jnp.float32),
            pltpu.VMEM((keys, HEAD_SIZE), jnp.float32),
            dma((DOC_SHARDS, KEY_VALUE_HEADS, 2)),
            dma((DOC_SHARDS, KEY_VALUE_HEADS, 2)),
            dma((DOC_SHARDS, KEY_VALUE_HEADS)),
            dma((DOC_SHARDS, KEY_VALUE_HEADS)),
            dma((shards,)),
            dma((shards, chips)),
            dma((shards, chips)),
            dma((shards, chips)),
            dma((shards, chips)),
            dma((shards, chips)),
            dma,
        ],
        compiler_params=pltpu.CompilerParams(
            vmem_limit_bytes=53*1024*1024, collective_id=0, has_side_effects=True
        ),
    )(lengths, query, grad, kv0, w_own)


def plan_of(shards):
    return {
        "start": (("kv", 0), ("kv", 1), ("kv", 2), ("own", 0), ("kv", 3),),
        "early": (("line", 1), ("line", 2),),
        (0, 2): (("line", 3), ("y", 0),),
        (1, 0): (("x", 0),),
        (1, 1): (("y", 1),),
        (1, 2): (("x", 1),),
        (2, 0): (("y", 2),),
        (2, 1): (("by", 1), ("py", 1), ("by", 2), ("py", 2),),
        (2, 3): (("y", 3), ("bx", 1), ("px", 1), ("x", 3), ("x", 2), ("bx", 2), ("px", 2), ("d", 0),),
        "after": (("d", 3), ("by", 3), ("py", 3), ("bd", 1), ("bd", 2), ("d", 2), ("pd", 2), ("bx", 3), ("px", 3), ("bd", 3), ("pd", 3), ("d", 1), ("pd", 1),),
    }


def plane_kernel(
    shape, plan, lengths, query_hbm, grad_hbm, kv_hbm, w_own, grad_query, grad_kv, w_all,
    query, grad, kv0, in_sem, kv_sem,
    window, near, far, landed_near, landed_far, own, rest, bias, dk, dv,
    kv_send, kv_recv, g_send, g_recv, line_send, line_recv, side_send, side_recv,
    diag_send, diag_recv, tail_send, tail_recv, pair_send, pair_recv, local_sem,
):
    shards, count = shape
    chips = count // 2
    rows = query.shape[0]
    half = rows // 2
    group_width = GROUP * HEAD_SIZE
    w_rows = w_own.shape[0]
    part_one = w_rows * 32 // 128
    part_two = w_rows * 80 // 128
    keys = (DOC_SHARDS + 1) * rows
    scale = HEAD_SIZE ** (-0.5)
    z = lax.axis_index("fsdp")
    me = lax.axis_index("ctx")
    core = lax.rem(me, 2)
    chip = me // 2
    x = lax.rem(chip, 2)
    y = chip // 2
    even = x == y
    x_peer = me + 2 - 4 * x
    y_peer = me + 4 - 8 * y
    d_peer = x_peer + 4 - 8 * y
    sides = (x_peer, y_peer, d_peer)
    partner = me + 1 - 2 * core
    has_prev = chip >= 1
    has_next = chip < chips - 1
    up = lax.rem(z + 1, shards)
    down = lax.rem(z - 1 + shards, shards)

    def query_in(g):
        cols = pl.ds(pl.multiple_of(g * group_width, HEAD_SIZE), group_width)
        return pltpu.make_async_copy(query_hbm.at[:, cols], query.at[:, cols], in_sem.at[0, g])

    def grad_in(g):
        cols = pl.ds(pl.multiple_of(g * group_width, HEAD_SIZE), group_width)
        return pltpu.make_async_copy(grad_hbm.at[:, cols], grad.at[:, cols], in_sem.at[1, g])

    kv_in = pltpu.make_async_copy(kv_hbm, kv0, kv_sem)
    kv_in.start()
    for g in range(KEY_VALUE_HEADS):
        query_in(g).start()
        grad_in(g).start()

    barrier = pltpu.get_barrier_semaphore()
    peers = [(z, partner), (z, x_peer), (z, y_peer), (z, d_peer), (up, me), (down, me)]
    for peer in peers:
        pl.semaphore_signal(barrier, inc=1, device_id=peer, device_id_type=pl.DeviceIdType.MESH)
    pl.semaphore_wait(barrier, len(peers))

    def remote(src, dst, send, recv, device):
        return pltpu.make_async_remote_copy(
            src_ref=src, dst_ref=dst, send_sem=send, recv_sem=recv,
            device_id=device, device_id_type=pl.DeviceIdType.MESH,
        )

    def kv_cols(g, part):
        return pl.ds(pl.multiple_of((part * KEY_VALUE_HEADS + g) * HEAD_SIZE, HEAD_SIZE), HEAD_SIZE)

    def kv_far(g, part):
        cols = kv_cols(g, part)
        return remote(
            kv_hbm.at[:, cols], window.at[1, :, cols], kv_send.at[1, g, part], kv_recv.at[1, g, part],
            (z, lax.rem(me + 2, count)),
        )

    def kv_near(g, part):
        cols = kv_cols(g, part)
        return remote(
            kv_hbm.at[:, cols], window.at[0, :, cols], kv_send.at[0, g, part], kv_recv.at[0, g, part],
            (z, partner),
        )

    def kv_relay(g, part):
        cols = kv_cols(g, part)
        return remote(
            window.at[1, :, cols], window.at[0, :, cols], kv_send.at[0, g, part], kv_recv.at[0, g, part],
            (z, partner),
        )

    def near_copy(g):
        return remote(near.at[g], landed_near.at[g], g_send.at[0, g], g_recv.at[0, g], (z, partner))

    def far_copy(g):
        return remote(
            far.at[g], landed_far.at[g], g_send.at[1, g], g_recv.at[1, g],
            (z, lax.rem(me - 2 + count, count)),
        )

    def block(zz, c, first=0, last=None):
        size = (w_rows if last is None else last) - first
        return w_all.at[pl.ds(pl.multiple_of((zz * count + c) * w_rows + first, 8), size)]

    def line(zz, way, mine=False):
        device = (up if way == 0 else down, me)
        return remote(
            w_own if mine else block(zz, me), block(zz, me), line_send.at[way, zz], line_recv.at[zz], device
        )

    def side(k, zz, mine=False):
        last = w_rows if mine else part_two
        src = w_own if mine else block(zz, me, 0, last)
        return remote(
            src, block(zz, me, 0, last), side_send.at[k, zz], side_recv.at[k, zz], (z, sides[k])
        )

    def side_wait(k, zz, whole):
        last = w_rows if whole else part_two
        ref = block(zz, sides[k], 0, last)
        remote(ref, ref, side_send.at[k, zz], side_recv.at[k, zz], (z, sides[k])).wait_recv()

    def diag_two(zz, whole):
        ref = block(zz, x_peer, part_one, w_rows if whole else part_two)
        return remote(ref, ref, diag_send.at[1, zz], diag_recv.at[1, zz], (z, y_peer))

    def diag_one(zz, over_x):
        ref = block(zz, y_peer if over_x else x_peer, 0, part_one)
        device = (z, x_peer if over_x else y_peer)
        return remote(ref, ref, diag_send.at[0, zz], diag_recv.at[0, zz], device)

    def diag_wait(zz, whole):
        ref = block(zz, d_peer, 0, part_one)
        remote(ref, ref, diag_send.at[0, zz], diag_recv.at[0, zz], (z, y_peer)).wait_recv()
        ref = block(zz, d_peer, part_one, w_rows if whole else part_two)
        remote(ref, ref, diag_send.at[1, zz], diag_recv.at[1, zz], (z, y_peer)).wait_recv()

    def tail(k, zz, way):
        ref = block(zz, sides[k], part_two, w_rows)
        device = (up if way == 0 else down, me)
        return remote(ref, ref, tail_send.at[way, k, zz], tail_recv.at[k, zz], device)

    def pair(k, zz, mine=False):
        ref = block(zz, me if k == 3 else sides[k])
        return remote(
            w_own if mine else ref, ref, pair_send.at[k, zz], pair_recv.at[k, zz], (z, partner)
        )

    shorter = jnp.minimum(z, shards - 1 - z)
    longer = jnp.where(z < shards - 1 - z, 1, -1)

    def source(i):
        near_side = i <= 2 * shorter
        sign = jnp.where(near_side, 1 if i % 2 == 1 else -1, longer)
        distance = jnp.where(near_side, (i + 1) // 2, i - shorter)
        return z + sign * distance, sign

    def start(copy):
        copy.start()

    def finish(copy):
        copy.wait_send()

    def onward(make, sign, act):
        @pl.when((sign < 0) & (z < shards - 1))
        def _():
            act(make(0))

        @pl.when((sign > 0) & (z > 0))
        def _():
            act(make(1))

    def both_ways(make, act):
        @pl.when(z < shards - 1)
        def _():
            act(make(0))

        @pl.when(z > 0)
        def _():
            act(make(1))

    def own_line(act):
        both_ways(lambda way: line(z, way, True), act)

    def relay_x(zz, whole, act):
        act(diag_two(zz, whole))

        @pl.when(jnp.logical_not(even))
        def _():
            act(diag_one(zz, False))

    def relay_y(zz, act):
        @pl.when(even)
        def _():
            act(diag_one(zz, True))

    def event(kind, i, wait, act):
        if kind == "kv":
            @pl.when(has_next)
            def _():
                for part in range(2):
                    act(kv_far(i, part))
            return
        if kind == "own":
            own_line(act)
            act(side(1, z, True))
            act(side(0, z, True))
            return
        zz, sign = (z, 0) if i == 0 else source(i)
        if kind == "line":
            if wait:
                remote(block(zz, me), block(zz, me), line_send.at[0, zz], line_recv.at[zz], (up, me)).wait_recv()
            onward(lambda way: line(zz, way), sign, act)
            act(side(1, zz))
            act(side(0, zz))
            act(pair(3, zz))
        elif kind == "x":
            if wait:
                side_wait(0, zz, i == 0)
            relay_x(zz, i == 0, act)
            if i == 0:
                both_ways(lambda way: tail(0, zz, way), act)
                act(pair(0, zz))
        elif kind == "y":
            if wait:
                side_wait(1, zz, i == 0)
            relay_y(zz, act)
            if i == 0:
                both_ways(lambda way: tail(1, zz, way), act)
                act(pair(1, zz))
        elif kind == "d":
            if wait:
                diag_wait(zz, i == 0)
            if i == 0:
                both_ways(lambda way: tail(2, zz, way), act)
                act(pair(2, zz))
        elif kind in ("bx", "by", "bd"):
            k = ("bx", "by", "bd").index(kind)
            if wait:
                ref = block(zz, sides[k], part_two, w_rows)
                remote(ref, ref, tail_send.at[0, k, zz], tail_recv.at[k, zz], (up, me)).wait_recv()
            onward(lambda way: tail(k, zz, way), sign, act)
        elif kind in ("px", "py", "pd"):
            act(pair(("px", "py", "pd").index(kind), zz))

    def serve(events):
        for kind, i in events:
            event(kind, i, True, start)

    def kv_forward(g):
        @pl.when(has_prev)
        def _():
            for part in range(2):
                kv_far(g, part).wait_recv()

        @pl.when(has_prev & (core == 1))
        def _():
            for part in range(2):
                kv_relay(g, part).start()

    serve(plan["start"])
    for g in range(KEY_VALUE_HEADS):
        @pl.when(core == 0)
        def _():
            for part in range(2):
                kv_near(g, part).start()
    pair(3, z, True).start()
    local = pltpu.make_async_copy(w_own, block(z, me), local_sem)
    local.start()

    @pl.when(me < 1)
    def _():
        window[0] = jnp.zeros(window.shape[1:], window.dtype)

    @pl.when(me < 2)
    def _():
        window[1] = jnp.zeros(window.shape[1:], window.dtype)

    first = me * rows
    pos = first + lax.broadcasted_iota(jnp.int32, (1, rows), 1)
    begin = jnp.zeros((1, rows), jnp.int32)
    end = jnp.int32(0)
    for d in range(lengths.shape[1]):
        end = end + lengths[0, d]
        begin = jnp.where(pos >= end, end, begin)
    key_pos = first - DOC_SHARDS * rows + lax.broadcasted_iota(jnp.int32, (keys, rows), 0)
    live = (key_pos >= begin) & (key_pos <= pos)
    bias[...] = jnp.where(live, 0.0, -1e30)

    def send_far(g):
        @pl.when(has_prev & (core == 1))
        def _():
            near_copy(g).wait_recv()
            for part in range(2):
                far[g, part] = (rest[part] + landed_near[g, part].astype(jnp.float32)).astype(jnp.bfloat16)

        @pl.when(has_prev & (core == 0))
        def _():
            for part in range(2):
                far[g, part] = rest[part].astype(jnp.bfloat16)

        @pl.when(has_prev)
        def _():
            far_copy(g).start()

    def blocks(a):
        return a[:half, :half], a[half:keys - half], a[keys - half:, half:]

    def joined(top, middle, bottom):
        empty = jnp.zeros((half, half), top.dtype)
        return jnp.concatenate(
            [jnp.concatenate([top, empty], axis=1), middle, jnp.concatenate([empty, bottom], axis=1)], axis=0
        )

    def column_sum(top, middle, bottom):
        total = jnp.sum(middle, axis=0, keepdims=True)
        return total + jnp.concatenate(
            [jnp.sum(top, axis=0, keepdims=True), jnp.sum(bottom, axis=0, keepdims=True)], axis=1
        )

    def split(row):
        return row[:, :half], row, row[:, half:]

    def heads(g, which, key, value):
        all_p, all_ds, all_q, all_go = [], [], [], []
        for h in which:
            cols = pl.ds(pl.multiple_of((g * GROUP + h) * HEAD_SIZE, HEAD_SIZE), HEAD_SIZE)
            q = query[:, cols]
            go = grad[:, cols]
            s = dot(key, q, ((1,), (1,)))
            dp = blocks(dot(value, go, ((1,), (1,))))
            b = (bias[:half, :half], bias[half:keys - half, :], bias[keys - half:, half:])
            e = [jnp.exp2(si * (scale * LOG2E) + bi) for si, bi in zip(blocks(s), b)]
            inv = 1.0 / column_sum(*e)
            delta = column_sum(*[ei * di for ei, di in zip(e, dp)]) * inv
            p = [ei * ii for ei, ii in zip(e, split(inv))]
            ds = [(pi * (di - li)).astype(jnp.bfloat16) for pi, di, li in zip(p, dp, split(delta))]
            all_p.append(joined(*[pi.astype(jnp.bfloat16) for pi in p]))
            all_ds.append(joined(*ds))
            all_q.append(q)
            all_go.append(go)
        p = jnp.concatenate(all_p, axis=1)
        ds = jnp.concatenate(all_ds, axis=1)
        return (
            dot(p, jnp.concatenate(all_go, axis=0), ((1,), (0,))),
            dot(ds, jnp.concatenate(all_q, axis=0), ((1,), (0,))),
            dot(key, ds, ((0,), (0,))),
        )

    def group(g, carry):
        @pl.when(me >= 1)
        def _():
            for part in range(2):
                kv_near(g, part).wait_recv()
        query_in(g).wait()
        grad_in(g).wait()

        kc = pl.ds(pl.multiple_of(g * HEAD_SIZE, HEAD_SIZE), HEAD_SIZE)
        vc = pl.ds(pl.multiple_of((g + KEY_VALUE_HEADS) * HEAD_SIZE, HEAD_SIZE), HEAD_SIZE)
        for n in range(0, GROUP, STEP):
            key = jnp.concatenate([window[1, :, kc], window[0, :, kc], kv0[:, kc]], axis=0)
            value = jnp.concatenate([window[1, :, vc], window[0, :, vc], kv0[:, vc]], axis=0)
            dv_part, dk_part, dq = heads(g, range(n, n + STEP), key, value)
            if n == 0:
                dv[...] = dv_part
                dk[...] = dk_part
            else:
                dv[...] += dv_part
                dk[...] += dk_part
            for j in range(STEP):
                cols = pl.ds(pl.multiple_of((g * GROUP + n + j) * HEAD_SIZE, HEAD_SIZE), HEAD_SIZE)
                grad_query[:, cols] = (dq[:, j * rows:(j + 1) * rows] * scale).T.astype(jnp.bfloat16)
            if n == 0:
                @pl.when(g >= 1)
                def _():
                    send_far(g - 1)
            if n == GROUP - STEP:
                @pl.when(g < KEY_VALUE_HEADS - 1)
                def _():
                    kv_forward(g + 1)
            for k in range(KEY_VALUE_HEADS):
                events = plan.get((k, n // STEP), ())
                if events:
                    @pl.when(g == k)
                    def _():
                        serve(events)
        near[g, 0] = (dk[rows:2 * rows, :] * scale).astype(jnp.bfloat16)
        near[g, 1] = dv[rows:2 * rows, :].astype(jnp.bfloat16)

        @pl.when(me >= 1)
        def _():
            near_copy(g).start()
        rest[0] = dk[:rows, :] * scale
        rest[1] = dv[:rows, :]
        own[g, 0] = dk[2 * rows:, :] * scale
        own[g, 1] = dv[2 * rows:, :]
        return carry

    serve(plan["early"])
    kv_forward(0)
    kv_in.wait()
    lax.fori_loop(0, KEY_VALUE_HEADS, group, 0)
    send_far(KEY_VALUE_HEADS - 1)
    serve(plan["after"])

    for g in range(KEY_VALUE_HEADS):
        @pl.when(core == 0)
        def _():
            near_copy(g).wait_recv()
            for part in range(2):
                own[g, part] += landed_near[g, part].astype(jnp.float32)

        @pl.when(has_next)
        def _():
            far_copy(g).wait_recv()
            for part in range(2):
                own[g, part] += landed_far[g, part].astype(jnp.float32)
        for part in range(2):
            at = (part * KEY_VALUE_HEADS + g) * HEAD_SIZE
            grad_kv[:, at:at + HEAD_SIZE] = own[g, part].astype(jnp.bfloat16)

    for k in range(4):
        for zz in range(shards):
            ref = block(zz, partner if k == 3 else sides[k] + 1 - 2 * core)
            remote(ref, ref, pair_send.at[k, zz], pair_recv.at[k, zz], (z, partner)).wait_recv()

    pair(3, z, True).wait_send()
    for events in plan.values():
        for kind, i in events:
            event(kind, i, False, finish)
    local.wait()
    for g in range(KEY_VALUE_HEADS):
        for part in range(2):
            @pl.when(core == 0)
            def _():
                kv_near(g, part).wait_send()

            @pl.when(has_prev & (core == 1))
            def _():
                kv_relay(g, part).wait_send()

        @pl.when(me >= 1)
        def _():
            near_copy(g).wait_send()

        @pl.when(has_prev)
        def _():
            far_copy(g).wait_send()


def plane_gradients(shape, lengths, query, grad, kv0, w_own):
    rows, width = query.shape
    keys = (DOC_SHARDS + 1) * rows
    w_rows, columns = w_own.shape
    shards, count = shape
    dma = pltpu.SemaphoreType.DMA
    terms = (KEY_VALUE_HEADS, 2, rows, HEAD_SIZE)
    operands = [pltpu.with_memory_space_constraint(a, pltpu.HBM) for a in (query, grad, kv0, w_own)]
    return pl.pallas_call(
        functools.partial(plane_kernel, shape, plan_of(shards)),
        in_specs=[pl.BlockSpec(memory_space=pltpu.SMEM)] + [pl.BlockSpec(memory_space=pltpu.HBM)] * 4,
        out_specs=[pl.BlockSpec(memory_space=pltpu.VMEM)] * 3,
        out_shape=[
            pltpu.VMEM((rows, width), jnp.bfloat16),
            pltpu.VMEM((rows, columns), jnp.bfloat16),
            pltpu.VMEM((w_rows * shards * count, columns), jnp.bfloat16),
        ],
        scratch_shapes=[
            pltpu.VMEM((rows, width), jnp.bfloat16),
            pltpu.VMEM((rows, width), jnp.bfloat16),
            pltpu.VMEM((rows, columns), jnp.bfloat16),
            dma((2, KEY_VALUE_HEADS)),
            dma,
            pltpu.VMEM((DOC_SHARDS, rows, columns), jnp.bfloat16),
            pltpu.VMEM(terms, jnp.bfloat16),
            pltpu.VMEM(terms, jnp.bfloat16),
            pltpu.VMEM(terms, jnp.bfloat16),
            pltpu.VMEM(terms, jnp.bfloat16),
            pltpu.VMEM(terms, jnp.float32),
            pltpu.VMEM(terms[1:], jnp.float32),
            pltpu.VMEM((keys, rows), jnp.float32),
            pltpu.VMEM((keys, HEAD_SIZE), jnp.float32),
            pltpu.VMEM((keys, HEAD_SIZE), jnp.float32),
            dma((DOC_SHARDS, KEY_VALUE_HEADS, 2)),
            dma((DOC_SHARDS, KEY_VALUE_HEADS, 2)),
            dma((2, KEY_VALUE_HEADS)),
            dma((2, KEY_VALUE_HEADS)),
            dma((2, shards)),
            dma((shards,)),
            dma((2, shards)),
            dma((2, shards)),
            dma((2, shards)),
            dma((2, shards)),
            dma((2, 3, shards)),
            dma((3, shards)),
            dma((4, shards)),
            dma((4, shards)),
            dma,
        ],
        compiler_params=pltpu.CompilerParams(
            vmem_limit_bytes=50 * 1024 * 1024, collective_id=1, has_side_effects=True
        ),
    )(lengths, *operands)


def finish_kernel(q_ref, kv_ref, w_ref, q_out, kv_out, in_out, buf, sems):
    chunks = sems.shape[0] - 2
    step = buf.shape[1] // chunks
    qc = pltpu.make_async_copy(q_ref, q_out, sems.at[chunks])
    kc = pltpu.make_async_copy(kv_ref, kv_out, sems.at[chunks + 1])
    qc.start()
    kc.start()
    def cp(n):
        cols = pl.ds(n * step, step)
        return pltpu.make_async_copy(buf.at[:, cols], in_out.at[:, cols], sems.at[n])
    for n in range(chunks):
        buf[:, n * step:(n + 1) * step] = dot(kv_ref[...], w_ref[n * step:(n + 1) * step, :], ((1,), (1,))).astype(jnp.bfloat16)
        cp(n).start()
    for n in range(chunks):
        cp(n).wait()
    qc.wait()
    kc.wait()


def finish(grad_query, grad_kv, weight):
    rows, width = grad_query.shape
    feats = weight.shape[0]
    anyspec = pl.BlockSpec(memory_space=pl.ANY)
    vm = pl.BlockSpec(memory_space=pltpu.VMEM)
    return pl.pallas_call(
        finish_kernel,
        in_specs=[vm, vm, vm],
        out_specs=[anyspec] * 3,
        out_shape=[
            jax.ShapeDtypeStruct((rows, width), jnp.bfloat16),
            jax.ShapeDtypeStruct(grad_kv.shape, jnp.bfloat16),
            jax.ShapeDtypeStruct((rows, feats), jnp.bfloat16),
        ],
        scratch_shapes=[pltpu.VMEM((rows, feats), jnp.bfloat16), pltpu.SemaphoreType.DMA((10,))],
        compiler_params=pltpu.CompilerParams(vmem_limit_bytes=20*1024*1024),
    )(grad_query, grad_kv, weight)


def body(query, key_value_rows, grad_out, doc_lengths, key_value_weight):
    shape = (lax.axis_size("fsdp"), lax.axis_size("ctx"))
    run = plane_gradients if shape[0] == 4 and shape[1] == 8 else gradients
    grad_query, grad_kv, weight = run(
        shape, doc_lengths, query[0], grad_out[0], key_value_rows[0], key_value_weight
    )
    grad_query, grad_kv, grad_input = finish(grad_query, grad_kv, weight)
    return (grad_query[None], grad_kv[None], grad_input[None])


def solution(mesh):
    in_specs = (
        P("fsdp", "ctx", None),
        P("fsdp", "ctx", None),
        P("fsdp", "ctx", None),
        P("fsdp", None),
        P(("fsdp", "ctx"), None),
    )
    out_specs = (P("fsdp", "ctx", None), P("fsdp", "ctx", None), P("fsdp", "ctx", None))
    return jax.shard_map(body, mesh=mesh, in_specs=in_specs, out_specs=out_specs, check_vma=False)
```

```python
import functools

import jax
import jax.numpy as jnp
from jax import lax
from jax.experimental import pallas as pl
from jax.experimental.pallas import tpu as pltpu
from jax.sharding import PartitionSpec as P

QUERY_HEAD_COUNT = 32
KEY_VALUE_HEADS = 4
HEAD_SIZE = 128
DOC_SHARDS = 2
GROUP = QUERY_HEAD_COUNT // KEY_VALUE_HEADS
STEP = 2
LOG2E = 1.4426950408889634


def dot(a, b, dims):
    return lax.dot_general(a, b, (dims, ((), ())), preferred_element_type=jnp.float32)


def gradients_kernel(
    shape, lengths, query_hbm, grad_hbm, kv_hbm, w_own, grad_query, grad_kv, w_all,
    query, grad, kv0, in_sem, kv_sem,
    window, staged, landed, own, bias, dk, dv,
    kv_send, kv_recv, g_send, g_recv, z_send, r_send, l_send, p_send, w_recv, p_recv, local_sem,
):
    shards, count = shape
    chips = count // 2
    half = chips // 2
    width = int(chips ** 0.5)
    rows = query.shape[0]
    group_width = GROUP * HEAD_SIZE
    w_rows = w_own.shape[0]
    keys = (DOC_SHARDS + 1) * rows
    scale = HEAD_SIZE ** (-0.5)
    z = lax.axis_index("fsdp")
    me = lax.axis_index("ctx")
    core = lax.rem(me, 2)
    chip = me // 2
    line = chip // width
    column = lax.rem(chip, width)
    odd = lax.rem(line, 2)
    place = line * width + column + odd * (width - 1 - 2 * column)

    def ring_ctx(spot):
        spot = lax.rem(spot + chips, chips)
        row = spot // width
        col = lax.rem(spot, width)
        return 2 * (row * width + col + lax.rem(row, 2) * (width - 1 - 2 * col)) + core

    right = ring_ctx(place + 1)
    left = ring_ctx(place - 1)
    partner = me + 1 - 2 * core

    def query_in(g):
        cols = pl.ds(pl.multiple_of(g * group_width, HEAD_SIZE), group_width)
        return pltpu.make_async_copy(query_hbm.at[:, cols], query.at[:, cols], in_sem.at[0, g])

    def grad_in(g):
        cols = pl.ds(pl.multiple_of(g * group_width, HEAD_SIZE), group_width)
        return pltpu.make_async_copy(grad_hbm.at[:, cols], grad.at[:, cols], in_sem.at[1, g])

    kv_in = pltpu.make_async_copy(kv_hbm, kv0, kv_sem)
    kv_in.start()
    for g in range(KEY_VALUE_HEADS):
        query_in(g).start()
        grad_in(g).start()

    barrier = pltpu.get_barrier_semaphore()
    peers = [(z, lax.rem(me + o + count, count)) for o in (1, 2, -1, -2)]
    peers += [(lax.rem(z + r, shards), me) for r in range(1, shards)]
    peers += [(z, right), (z, left), (z, partner)]
    for peer in peers:
        pl.semaphore_signal(barrier, inc=1, device_id=peer, device_id_type=pl.DeviceIdType.MESH)
    pl.semaphore_wait(barrier, len(peers))

    def remote(src, dst, send, recv, device):
        return pltpu.make_async_remote_copy(
            src_ref=src, dst_ref=dst, send_sem=send, recv_sem=recv,
            device_id=device, device_id_type=pl.DeviceIdType.MESH,
        )

    def kv_copy(o, g, part):
        cols = pl.ds(pl.multiple_of((part * KEY_VALUE_HEADS + g) * HEAD_SIZE, HEAD_SIZE), HEAD_SIZE)
        return remote(
            kv_hbm.at[:, cols], window.at[o, :, cols], kv_send.at[o, g, part], kv_recv.at[o, g, part],
            (z, lax.rem(me + o + 1, count)),
        )

    def kv_relay(g, part):
        cols = pl.ds(pl.multiple_of((part * KEY_VALUE_HEADS + g) * HEAD_SIZE, HEAD_SIZE), HEAD_SIZE)
        return remote(
            window.at[1, :, cols], window.at[0, :, cols], kv_send.at[0, g, part], kv_recv.at[0, g, part],
            (z, partner),
        )

    sends_kv = [core == 0, me + 2 < count]
    relays_kv = (core == 1) & (me >= 2)

    def grad_copy(o, g):
        return remote(
            staged.at[o, g], landed.at[o, g], g_send.at[o, g], g_recv.at[o, g],
            (z, lax.rem(me - o - 1 + count, count)),
        )

    def block(zz, spot, flip=False):
        at = ring_ctx(spot)
        if flip:
            at = at + 1 - 2 * core
        return w_all.at[pl.ds(pl.multiple_of((zz * count + at) * w_rows, w_rows), w_rows)]

    def w_copy(zz, spot, sems, arrive, device, mine=False):
        spot = lax.rem(spot + chips, chips)
        src = w_own if mine else block(zz, spot)
        return remote(src, block(zz, spot), sems.at[zz, spot], arrive.at[zz, spot], device)

    def shard(r):
        return lax.rem(z - r + shards, shards)

    def w_arrived(r, t):
        w_copy(shard(r), place + t, r_send, w_recv, (z, right)).wait_recv()

    def takes_right(spot, zz):
        at = lax.rem(lax.rem(spot + chips, chips), 4)
        turn = lax.rem(zz, 4)
        even = lax.rem(at, 2) == 0
        return even | ((at == 1) & (turn >= 1)) | ((at == 3) & (turn >= 2))

    def each_copy(r, t, act):
        zz = shard(r)
        mine = r == 0 and t == 0
        if t == 0:
            act(w_copy(zz, place, r_send, w_recv, (z, right), mine))
            act(w_copy(zz, place, l_send, w_recv, (z, left), mine))
        elif -half + 1 <= t < 0:
            copy = w_copy(zz, place + t, r_send, w_recv, (z, right))
            if t > -half + 1:
                act(copy)
            else:
                pl.when(takes_right(place + 1, zz))(lambda: act(copy))
        elif 0 < t <= half - 1:
            copy = w_copy(zz, place + t, l_send, w_recv, (z, left))
            if t < half - 1:
                act(copy)
            else:
                pl.when(jnp.logical_not(takes_right(place - 1, zz)))(lambda: act(copy))
        act(w_copy(zz, place + t, p_send, p_recv, (z, partner), mine))

    def z_copy(r):
        to = lax.rem(z + r, shards)
        return remote(w_own, block(z, place), z_send.at[to], w_recv.at[z, place], (to, me))

    for g in range(KEY_VALUE_HEADS):
        for o in range(DOC_SHARDS):
            @pl.when(sends_kv[o])
            def _():
                kv_copy(o, g, 0).start()
                kv_copy(o, g, 1).start()

    for r in range(1, shards):
        z_copy(r).start()
    each_copy(0, 0, lambda c: c.start())
    local = pltpu.make_async_copy(w_own, block(z, place), local_sem)
    local.start()

    for o in range(DOC_SHARDS):
        @pl.when(me < o + 1)
        def _():
            window[o] = jnp.zeros(window.shape[1:], window.dtype)

        @pl.when(me + o + 1 >= count)
        def _():
            landed[o] = jnp.zeros(landed.shape[1:], landed.dtype)

    first = me * rows
    pos = first + lax.broadcasted_iota(jnp.int32, (1, rows), 1)
    start = jnp.zeros((1, rows), jnp.int32)
    end = jnp.int32(0)
    for d in range(lengths.shape[1]):
        end = end + lengths[0, d]
        start = jnp.where(pos >= end, end, start)
    key_pos = first - DOC_SHARDS * rows + lax.broadcasted_iota(jnp.int32, (keys, rows), 0)
    live = (key_pos >= start) & (key_pos <= pos)
    bias[...] = jnp.where(live, 0.0, -1e30)

    def group(g, carry):
        for o in reversed(range(DOC_SHARDS)):
            @pl.when(me >= o + 1)
            def _():
                kv_copy(o, g, 0).wait_recv()
                kv_copy(o, g, 1).wait_recv()

            if o == 1:
                @pl.when(relays_kv)
                def _():
                    kv_relay(g, 0).start()
                    kv_relay(g, 1).start()
        query_in(g).wait()
        grad_in(g).wait()

        @pl.when(g == 0)
        def _():
            kv_in.wait()
        kc = pl.ds(pl.multiple_of(g * HEAD_SIZE, HEAD_SIZE), HEAD_SIZE)
        vc = pl.ds(pl.multiple_of((g + KEY_VALUE_HEADS) * HEAD_SIZE, HEAD_SIZE), HEAD_SIZE)
        key = jnp.concatenate([window[1, :, kc], window[0, :, kc], kv0[:, kc]], axis=0)
        value = jnp.concatenate([window[1, :, vc], window[0, :, vc], kv0[:, vc]], axis=0)
        dk[...] = jnp.zeros_like(dk)
        dv[...] = jnp.zeros_like(dv)
        for h in range(GROUP):
            cols = pl.ds(pl.multiple_of((g * GROUP + h) * HEAD_SIZE, HEAD_SIZE), HEAD_SIZE)
            q = query[:, cols]
            go = grad[:, cols]
            s = dot(key, q, ((1,), (1,)))
            e = jnp.exp2(s * (scale * LOG2E) + bias[...])
            dp = dot(value, go, ((1,), (1,)))
            inv = 1.0 / jnp.sum(e, axis=0, keepdims=True)
            delta = jnp.sum(e * dp, axis=0, keepdims=True) * inv
            p = e * inv
            ds = (p * (dp - delta)).astype(jnp.bfloat16)
            dv[...] += dot(p.astype(jnp.bfloat16), go, ((1,), (0,)))
            dk[...] += dot(ds, q, ((1,), (0,)))
            dq = dot(key, ds, ((0,), (0,)))
            grad_query[:, cols] = (dq * scale).T.astype(jnp.bfloat16)
        for o in range(DOC_SHARDS):
            part = slice((DOC_SHARDS - 1 - o) * rows, (DOC_SHARDS - o) * rows)
            staged[o, g, 0] = (dk[part, :] * scale).astype(jnp.bfloat16)
            staged[o, g, 1] = dv[part, :].astype(jnp.bfloat16)
        own[g, 0] = dk[DOC_SHARDS * rows:, :] * scale
        own[g, 1] = dv[DOC_SHARDS * rows:, :]
        for o in range(DOC_SHARDS):
            @pl.when(me >= o + 1)
            def _():
                grad_copy(o, g).start()
        for k in range(KEY_VALUE_HEADS):
            turn = [r for r in range(1, shards) if min(r - 1, KEY_VALUE_HEADS - 1) == k]
            if turn:
                @pl.when(g == k)
                def _():
                    for r in turn:
                        w_arrived(r, 0)
                        each_copy(r, 0, lambda c: c.start())
        return carry

    lax.fori_loop(0, KEY_VALUE_HEADS, group, 0)

    for t in range(1, half):
        for r in range(shards):
            for side in (-t, t):
                w_arrived(r, side)
                each_copy(r, side, lambda c: c.start())

    for g in range(KEY_VALUE_HEADS):
        for o in range(DOC_SHARDS):
            @pl.when(me + o + 1 < count)
            def _():
                grad_copy(o, g).wait_recv()
        for part in range(2):
            total = own[g, part]
            for o in range(DOC_SHARDS):
                total = total + landed[o, g, part].astype(jnp.float32)
            at = (part * KEY_VALUE_HEADS + g) * HEAD_SIZE
            grad_kv[:, at:at + HEAD_SIZE] = total.astype(jnp.bfloat16)

    for r in range(shards):
        w_arrived(r, half)
        each_copy(r, half, lambda c: c.start())

    for r in range(shards):
        for t in range(-half + 1, half + 1):
            w_copy(shard(r), place + t, p_send, p_recv, (z, partner)).wait_recv()
            each_copy(r, t, lambda c: c.wait_send())
    for r in range(1, shards):
        z_copy(r).wait_send()
    local.wait()
    for g in range(KEY_VALUE_HEADS):
        @pl.when(relays_kv)
        def _():
            kv_relay(g, 0).wait_send()
            kv_relay(g, 1).wait_send()

        for o in range(DOC_SHARDS):
            @pl.when(sends_kv[o])
            def _():
                kv_copy(o, g, 0).wait_send()
                kv_copy(o, g, 1).wait_send()

            @pl.when(me >= o + 1)
            def _():
                grad_copy(o, g).wait_send()


def gradients(shape, lengths, query, grad, kv0, w_own):
    rows, width = query.shape
    keys = (DOC_SHARDS + 1) * rows
    w_rows, columns = w_own.shape
    shards, count = shape
    chips = count // 2
    vmem = pl.BlockSpec(memory_space=pltpu.VMEM)
    dma = pltpu.SemaphoreType.DMA
    parts = (DOC_SHARDS, KEY_VALUE_HEADS, 2, rows, HEAD_SIZE)
    return pl.pallas_call(
        functools.partial(gradients_kernel, shape),
        in_specs=[pl.BlockSpec(memory_space=pltpu.SMEM)] + [pl.BlockSpec(memory_space=pltpu.HBM)] * 4,
        out_specs=[pl.BlockSpec(memory_space=pltpu.VMEM)]*3,
        out_shape=[
            pltpu.VMEM((rows, width), jnp.bfloat16),
            pltpu.VMEM((rows, columns), jnp.bfloat16),
            pltpu.VMEM((w_rows * shards * count, columns), jnp.bfloat16),
        ],
        scratch_shapes=[
            pltpu.VMEM((rows, width), jnp.bfloat16),
            pltpu.VMEM((rows, width), jnp.bfloat16),
            pltpu.VMEM((rows, columns), jnp.bfloat16),
            dma((2, KEY_VALUE_HEADS)),
            dma,
            pltpu.VMEM((DOC_SHARDS, rows, columns), jnp.bfloat16),
            pltpu.VMEM(parts, jnp.bfloat16),
            pltpu.VMEM(parts, jnp.bfloat16),
            pltpu.VMEM(parts[1:], jnp.float32),
            pltpu.VMEM((keys, rows), jnp.float32),
            pltpu.VMEM((keys, HEAD_SIZE), jnp.float32),
            pltpu.VMEM((keys, HEAD_SIZE), jnp.float32),
            dma((DOC_SHARDS, KEY_VALUE_HEADS, 2)),
            dma((DOC_SHARDS, KEY_VALUE_HEADS, 2)),
            dma((DOC_SHARDS, KEY_VALUE_HEADS)),
            dma((DOC_SHARDS, KEY_VALUE_HEADS)),
            dma((shards,)),
            dma((shards, chips)),
            dma((shards, chips)),
            dma((shards, chips)),
            dma((shards, chips)),
            dma((shards, chips)),
            dma,
        ],
        compiler_params=pltpu.CompilerParams(
            vmem_limit_bytes=53*1024*1024, collective_id=0, has_side_effects=True
        ),
    )(lengths, query, grad, kv0, w_own)


def plan_of(shards):
    return {
        "start": (
            (("kv", 0), ("kv", 1), ("own", 0), ("kv", 2), ("kv", 3),),
            (("kv", 0), ("own", 0), ("kv", 1), ("kv", 2),),
        ),
        "early": (
            (("y", 0), ("line", 1), ("line", 2),),
            (("line", 1),),
        ),
        (0, 2): (
            (),
            (("y", 0), ("x", 0), ("kv", 3),),
        ),
        (0, 3): (
            (("x", 0),),
            (),
        ),
        (1, 1): (
            (("line", 3),),
            (),
        ),
        (1, 2): (
            (("bx", 2), ("by", 2),),
            (("line", 2),),
        ),
        (2, 0): (
            (("by", 1), ("x", 1),),
            (),
        ),
        (2, 1): (
            (("d", 0),),
            (("by", 1), ("x", 1), ("d", 0),),
        ),
        (2, 2): (
            (("y", 1), ("py", 1),),
            (("line", 3),),
        ),
        (2, 3): (
            (("bx", 1), ("px", 1),),
            (),
        ),
        (3, 0): (
            (("bd", 2), ("x", 2), ("px", 2), ("y", 2), ("py", 2), ("by", 3),),
            (),
        ),
        (3, 1): (
            (),
            (("x", 2), ("y", 1), ("py", 1),),
        ),
        (3, 2): (
            (("x", 3), ("y", 3), ("py", 3), ("bd", 1),),
            (),
        ),
        "after": (
            (("bx", 3), ("px", 3), ("bd", 3), ("d", 3), ("pd", 3), ("d", 1), ("pd", 1), ("d", 2), ("pd", 2),),
            (("by", 2), ("x", 3), ("y", 2), ("py", 2), ("y", 3), ("by", 3), ("py", 3), ("bx", 1), ("px", 1), ("d", 3), ("bx", 2), ("px", 2), ("bd", 1), ("bx", 3), ("px", 3), ("bd", 3), ("pd", 3), ("bd", 2), ("d", 2), ("pd", 2), ("d", 1), ("pd", 1),),
        ),
    }


def plane_kernel(
    shape, plan, lengths, query_hbm, grad_hbm, kv_hbm, w_own, grad_query, grad_kv, w_all,
    query, grad, kv0, in_sem, kv_sem,
    window, near, far, landed_near, landed_far, own, rest, bias, dk, dv,
    kv_send, kv_recv, g_send, g_recv, line_send, line_recv, side_send, side_recv,
    diag_send, diag_recv, tail_send, tail_recv, pair_send, pair_recv, local_sem,
):
    shards, count = shape
    chips = count // 2
    rows = query.shape[0]
    half = rows // 2
    group_width = GROUP * HEAD_SIZE
    w_rows = w_own.shape[0]
    part_one = w_rows * 56 // 128
    part_two = w_rows * 80 // 128
    keys = (DOC_SHARDS + 1) * rows
    scale = HEAD_SIZE ** (-0.5)
    z = lax.axis_index("fsdp")
    me = lax.axis_index("ctx")
    core = lax.rem(me, 2)
    chip = me // 2
    x = lax.rem(chip, 2)
    y = chip // 2
    even = x == y
    x_peer = me + 2 - 4 * x
    y_peer = me + 4 - 8 * y
    d_peer = x_peer + 4 - 8 * y
    sides = (x_peer, y_peer, d_peer)
    partner = me + 1 - 2 * core
    has_prev = chip >= 1
    has_next = chip < chips - 1
    up = lax.rem(z + 1, shards)
    down = lax.rem(z - 1 + shards, shards)

    def query_in(g):
        cols = pl.ds(pl.multiple_of(g * group_width, HEAD_SIZE), group_width)
        return pltpu.make_async_copy(query_hbm.at[:, cols], query.at[:, cols], in_sem.at[0, g])

    def grad_in(g):
        cols = pl.ds(pl.multiple_of(g * group_width, HEAD_SIZE), group_width)
        return pltpu.make_async_copy(grad_hbm.at[:, cols], grad.at[:, cols], in_sem.at[1, g])

    kv_in = pltpu.make_async_copy(kv_hbm, kv0, kv_sem)
    kv_in.start()
    for g in range(KEY_VALUE_HEADS):
        query_in(g).start()
        grad_in(g).start()

    barrier = pltpu.get_barrier_semaphore()
    peers = [(z, partner), (z, x_peer), (z, y_peer), (z, d_peer), (up, me), (down, me)]
    for peer in peers:
        pl.semaphore_signal(barrier, inc=1, device_id=peer, device_id_type=pl.DeviceIdType.MESH)
    pl.semaphore_wait(barrier, len(peers))

    def remote(src, dst, send, recv, device):
        return pltpu.make_async_remote_copy(
            src_ref=src, dst_ref=dst, send_sem=send, recv_sem=recv,
            device_id=device, device_id_type=pl.DeviceIdType.MESH,
        )

    def kv_cols(g, part):
        return pl.ds(pl.multiple_of((part * KEY_VALUE_HEADS + g) * HEAD_SIZE, HEAD_SIZE), HEAD_SIZE)

    def kv_far(g, part):
        cols = kv_cols(g, part)
        return remote(
            kv_hbm.at[:, cols], window.at[1, :, cols], kv_send.at[1, g, part], kv_recv.at[1, g, part],
            (z, lax.rem(me + 2, count)),
        )

    def kv_near(g, part):
        cols = kv_cols(g, part)
        return remote(
            kv_hbm.at[:, cols], window.at[0, :, cols], kv_send.at[0, g, part], kv_recv.at[0, g, part],
            (z, partner),
        )

    def kv_relay(g, part):
        cols = kv_cols(g, part)
        return remote(
            window.at[1, :, cols], window.at[0, :, cols], kv_send.at[0, g, part], kv_recv.at[0, g, part],
            (z, partner),
        )

    def near_copy(g):
        return remote(near.at[g], landed_near.at[g], g_send.at[0, g], g_recv.at[0, g], (z, partner))

    def far_copy(g):
        return remote(
            far.at[g], landed_far.at[g], g_send.at[1, g], g_recv.at[1, g],
            (z, lax.rem(me - 2 + count, count)),
        )

    def block(zz, c, first=0, last=None):
        size = (w_rows if last is None else last) - first
        return w_all.at[pl.ds(pl.multiple_of((zz * count + c) * w_rows + first, 8), size)]

    def line(zz, way, mine=False):
        device = (up if way == 0 else down, me)
        return remote(
            w_own if mine else block(zz, me), block(zz, me), line_send.at[way, zz], line_recv.at[zz], device
        )

    def side(k, zz, mine=False):
        last = w_rows if mine else part_two
        src = w_own if mine else block(zz, me, 0, last)
        return remote(
            src, block(zz, me, 0, last), side_send.at[k, zz], side_recv.at[k, zz], (z, sides[k])
        )

    def side_wait(k, zz, whole):
        last = w_rows if whole else part_two
        ref = block(zz, sides[k], 0, last)
        remote(ref, ref, side_send.at[k, zz], side_recv.at[k, zz], (z, sides[k])).wait_recv()

    def diag_two(zz, whole):
        ref = block(zz, x_peer, part_one, w_rows if whole else part_two)
        return remote(ref, ref, diag_send.at[1, zz], diag_recv.at[1, zz], (z, y_peer))

    def diag_one(zz, over_x):
        ref = block(zz, y_peer if over_x else x_peer, 0, part_one)
        device = (z, x_peer if over_x else y_peer)
        return remote(ref, ref, diag_send.at[0, zz], diag_recv.at[0, zz], device)

    def diag_wait(zz, whole):
        ref = block(zz, d_peer, 0, part_one)
        remote(ref, ref, diag_send.at[0, zz], diag_recv.at[0, zz], (z, y_peer)).wait_recv()
        ref = block(zz, d_peer, part_one, w_rows if whole else part_two)
        remote(ref, ref, diag_send.at[1, zz], diag_recv.at[1, zz], (z, y_peer)).wait_recv()

    def tail(k, zz, way):
        ref = block(zz, sides[k], part_two, w_rows)
        device = (up if way == 0 else down, me)
        return remote(ref, ref, tail_send.at[way, k, zz], tail_recv.at[k, zz], device)

    def pair(k, zz, mine=False):
        ref = block(zz, me if k == 3 else sides[k])
        return remote(
            w_own if mine else ref, ref, pair_send.at[k, zz], pair_recv.at[k, zz], (z, partner)
        )

    shorter = jnp.minimum(z, shards - 1 - z)
    longer = jnp.where(z < shards - 1 - z, 1, -1)

    def source(i):
        near_side = i <= 2 * shorter
        sign = jnp.where(near_side, 1 if i % 2 == 1 else -1, longer)
        distance = jnp.where(near_side, (i + 1) // 2, i - shorter)
        return z + sign * distance, sign

    def start(copy):
        copy.start()

    def finish(copy):
        copy.wait_send()

    def onward(make, sign, act):
        @pl.when((sign < 0) & (z < shards - 1))
        def _():
            act(make(0))

        @pl.when((sign > 0) & (z > 0))
        def _():
            act(make(1))

    def both_ways(make, act):
        @pl.when(z < shards - 1)
        def _():
            act(make(0))

        @pl.when(z > 0)
        def _():
            act(make(1))

    def own_line(act):
        both_ways(lambda way: line(z, way, True), act)

    def relay_x(zz, whole, act):
        act(diag_two(zz, whole))

        @pl.when(jnp.logical_not(even))
        def _():
            act(diag_one(zz, False))

    def relay_y(zz, act):
        @pl.when(even)
        def _():
            act(diag_one(zz, True))

    def event(kind, i, wait, act):
        if kind == "kv":
            @pl.when(has_next)
            def _():
                for part in range(2):
                    act(kv_far(i, part))
            return
        if kind == "own":
            own_line(act)
            act(side(1, z, True))
            act(side(0, z, True))
            return
        zz, sign = (z, 0) if i == 0 else source(i)
        if kind == "line":
            if wait:
                remote(block(zz, me), block(zz, me), line_send.at[0, zz], line_recv.at[zz], (up, me)).wait_recv()
            onward(lambda way: line(zz, way), sign, act)
            act(side(1, zz))
            act(side(0, zz))
            act(pair(3, zz))
        elif kind == "x":
            if wait:
                side_wait(0, zz, i == 0)
            relay_x(zz, i == 0, act)
            if i == 0:
                both_ways(lambda way: tail(0, zz, way), act)
                act(pair(0, zz))
        elif kind == "y":
            if wait:
                side_wait(1, zz, i == 0)
            relay_y(zz, act)
            if i == 0:
                both_ways(lambda way: tail(1, zz, way), act)
                act(pair(1, zz))
        elif kind == "d":
            if wait:
                diag_wait(zz, i == 0)
            if i == 0:
                both_ways(lambda way: tail(2, zz, way), act)
                act(pair(2, zz))
        elif kind in ("bx", "by", "bd"):
            k = ("bx", "by", "bd").index(kind)
            if wait:
                ref = block(zz, sides[k], part_two, w_rows)
                remote(ref, ref, tail_send.at[0, k, zz], tail_recv.at[k, zz], (up, me)).wait_recv()
            onward(lambda way: tail(k, zz, way), sign, act)
        elif kind in ("px", "py", "pd"):
            act(pair(("px", "py", "pd").index(kind), zz))

    at_end = (z == 0) | (z == shards - 1)

    def serve(key, now=True):
        for place, events in zip((jnp.logical_not(at_end), at_end), plan.get(key, ((), ()))):
            if events:
                @pl.when(place & now)
                def _():
                    for kind, i in events:
                        event(kind, i, True, start)

    def kv_forward(g):
        @pl.when(has_prev)
        def _():
            for part in range(2):
                kv_far(g, part).wait_recv()

        @pl.when(has_prev & (core == 1))
        def _():
            for part in range(2):
                kv_relay(g, part).start()

    serve("start")
    for g in range(KEY_VALUE_HEADS):
        @pl.when(core == 0)
        def _():
            for part in range(2):
                kv_near(g, part).start()
    pair(3, z, True).start()
    local = pltpu.make_async_copy(w_own, block(z, me), local_sem)
    local.start()

    @pl.when(me < 1)
    def _():
        window[0] = jnp.zeros(window.shape[1:], window.dtype)

    @pl.when(me < 2)
    def _():
        window[1] = jnp.zeros(window.shape[1:], window.dtype)

    first = me * rows
    pos = first + lax.broadcasted_iota(jnp.int32, (1, rows), 1)
    begin = jnp.zeros((1, rows), jnp.int32)
    end = jnp.int32(0)
    for d in range(lengths.shape[1]):
        end = end + lengths[0, d]
        begin = jnp.where(pos >= end, end, begin)
    key_pos = first - DOC_SHARDS * rows + lax.broadcasted_iota(jnp.int32, (keys, rows), 0)
    live = (key_pos >= begin) & (key_pos <= pos)
    bias[...] = jnp.where(live, 0.0, -1e30)

    def send_far(g):
        @pl.when(has_prev & (core == 1))
        def _():
            near_copy(g).wait_recv()
            for part in range(2):
                far[g, part] = (rest[part] + landed_near[g, part].astype(jnp.float32)).astype(jnp.bfloat16)

        @pl.when(has_prev & (core == 0))
        def _():
            for part in range(2):
                far[g, part] = rest[part].astype(jnp.bfloat16)

        @pl.when(has_prev)
        def _():
            far_copy(g).start()

    def blocks(a):
        return a[:half, :half], a[half:keys - half], a[keys - half:, half:]

    def joined(top, middle, bottom):
        empty = jnp.zeros((half, half), top.dtype)
        return jnp.concatenate(
            [jnp.concatenate([top, empty], axis=1), middle, jnp.concatenate([empty, bottom], axis=1)], axis=0
        )

    def column_sum(top, middle, bottom):
        total = jnp.sum(middle, axis=0, keepdims=True)
        return total + jnp.concatenate(
            [jnp.sum(top, axis=0, keepdims=True), jnp.sum(bottom, axis=0, keepdims=True)], axis=1
        )

    def split(row):
        return row[:, :half], row, row[:, half:]

    def heads(g, which, key, value):
        all_p, all_ds, all_q, all_go = [], [], [], []
        for h in which:
            cols = pl.ds(pl.multiple_of((g * GROUP + h) * HEAD_SIZE, HEAD_SIZE), HEAD_SIZE)
            q = query[:, cols]
            go = grad[:, cols]
            s = dot(key, q, ((1,), (1,)))
            dp = blocks(dot(value, go, ((1,), (1,))))
            b = (bias[:half, :half], bias[half:keys - half, :], bias[keys - half:, half:])
            e = [jnp.exp2(si * (scale * LOG2E) + bi) for si, bi in zip(blocks(s), b)]
            inv = 1.0 / column_sum(*e)
            delta = column_sum(*[ei * di for ei, di in zip(e, dp)]) * inv
            p = [ei * ii for ei, ii in zip(e, split(inv))]
            ds = [(pi * (di - li)).astype(jnp.bfloat16) for pi, di, li in zip(p, dp, split(delta))]
            all_p.append(joined(*[pi.astype(jnp.bfloat16) for pi in p]))
            all_ds.append(joined(*ds))
            all_q.append(q)
            all_go.append(go)
        p = jnp.concatenate(all_p, axis=1)
        ds = jnp.concatenate(all_ds, axis=1)
        return (
            dot(p, jnp.concatenate(all_go, axis=0), ((1,), (0,))),
            dot(ds, jnp.concatenate(all_q, axis=0), ((1,), (0,))),
            dot(key, ds, ((0,), (0,))),
        )

    def group(g, carry):
        @pl.when(me >= 1)
        def _():
            for part in range(2):
                kv_near(g, part).wait_recv()
        query_in(g).wait()
        grad_in(g).wait()

        kc = pl.ds(pl.multiple_of(g * HEAD_SIZE, HEAD_SIZE), HEAD_SIZE)
        vc = pl.ds(pl.multiple_of((g + KEY_VALUE_HEADS) * HEAD_SIZE, HEAD_SIZE), HEAD_SIZE)
        for n in range(0, GROUP, STEP):
            key = jnp.concatenate([window[1, :, kc], window[0, :, kc], kv0[:, kc]], axis=0)
            value = jnp.concatenate([window[1, :, vc], window[0, :, vc], kv0[:, vc]], axis=0)
            dv_part, dk_part, dq = heads(g, range(n, n + STEP), key, value)
            if n == 0:
                dv[...] = dv_part
                dk[...] = dk_part
            else:
                dv[...] += dv_part
                dk[...] += dk_part
            for j in range(STEP):
                cols = pl.ds(pl.multiple_of((g * GROUP + n + j) * HEAD_SIZE, HEAD_SIZE), HEAD_SIZE)
                grad_query[:, cols] = (dq[:, j * rows:(j + 1) * rows] * scale).T.astype(jnp.bfloat16)
            if n == 0:
                @pl.when(g >= 1)
                def _():
                    send_far(g - 1)
            if n == GROUP - STEP:
                @pl.when(g < KEY_VALUE_HEADS - 1)
                def _():
                    kv_forward(g + 1)
            for k in range(KEY_VALUE_HEADS):
                serve((k, n // STEP), g == k)
        near[g, 0] = (dk[rows:2 * rows, :] * scale).astype(jnp.bfloat16)
        near[g, 1] = dv[rows:2 * rows, :].astype(jnp.bfloat16)

        @pl.when(me >= 1)
        def _():
            near_copy(g).start()
        rest[0] = dk[:rows, :] * scale
        rest[1] = dv[:rows, :]
        own[g, 0] = dk[2 * rows:, :] * scale
        own[g, 1] = dv[2 * rows:, :]
        return carry

    serve("early")
    kv_forward(0)
    kv_in.wait()
    lax.fori_loop(0, KEY_VALUE_HEADS, group, 0)
    send_far(KEY_VALUE_HEADS - 1)
    serve("after")

    for g in range(KEY_VALUE_HEADS):
        @pl.when(core == 0)
        def _():
            near_copy(g).wait_recv()
            for part in range(2):
                own[g, part] += landed_near[g, part].astype(jnp.float32)

        @pl.when(has_next)
        def _():
            far_copy(g).wait_recv()
            for part in range(2):
                own[g, part] += landed_far[g, part].astype(jnp.float32)
        for part in range(2):
            at = (part * KEY_VALUE_HEADS + g) * HEAD_SIZE
            grad_kv[:, at:at + HEAD_SIZE] = own[g, part].astype(jnp.bfloat16)

    for k in range(4):
        for zz in range(shards):
            ref = block(zz, partner if k == 3 else sides[k] + 1 - 2 * core)
            remote(ref, ref, pair_send.at[k, zz], pair_recv.at[k, zz], (z, partner)).wait_recv()

    pair(3, z, True).wait_send()
    for events, _ in plan.values():
        for kind, i in events:
            event(kind, i, False, finish)
    local.wait()
    for g in range(KEY_VALUE_HEADS):
        for part in range(2):
            @pl.when(core == 0)
            def _():
                kv_near(g, part).wait_send()

            @pl.when(has_prev & (core == 1))
            def _():
                kv_relay(g, part).wait_send()

        @pl.when(me >= 1)
        def _():
            near_copy(g).wait_send()

        @pl.when(has_prev)
        def _():
            far_copy(g).wait_send()


def plane_gradients(shape, lengths, query, grad, kv0, w_own):
    rows, width = query.shape
    keys = (DOC_SHARDS + 1) * rows
    w_rows, columns = w_own.shape
    shards, count = shape
    dma = pltpu.SemaphoreType.DMA
    terms = (KEY_VALUE_HEADS, 2, rows, HEAD_SIZE)
    operands = [pltpu.with_memory_space_constraint(a, pltpu.HBM) for a in (query, grad, kv0, w_own)]
    return pl.pallas_call(
        functools.partial(plane_kernel, shape, plan_of(shards)),
        in_specs=[pl.BlockSpec(memory_space=pltpu.SMEM)] + [pl.BlockSpec(memory_space=pltpu.HBM)] * 4,
        out_specs=[pl.BlockSpec(memory_space=pltpu.VMEM)] * 3,
        out_shape=[
            pltpu.VMEM((rows, width), jnp.bfloat16),
            pltpu.VMEM((rows, columns), jnp.bfloat16),
            pltpu.VMEM((w_rows * shards * count, columns), jnp.bfloat16),
        ],
        scratch_shapes=[
            pltpu.VMEM((rows, width), jnp.bfloat16),
            pltpu.VMEM((rows, width), jnp.bfloat16),
            pltpu.VMEM((rows, columns), jnp.bfloat16),
            dma((2, KEY_VALUE_HEADS)),
            dma,
            pltpu.VMEM((DOC_SHARDS, rows, columns), jnp.bfloat16),
            pltpu.VMEM(terms, jnp.bfloat16),
            pltpu.VMEM(terms, jnp.bfloat16),
            pltpu.VMEM(terms, jnp.bfloat16),
            pltpu.VMEM(terms, jnp.bfloat16),
            pltpu.VMEM(terms, jnp.float32),
            pltpu.VMEM(terms[1:], jnp.float32),
            pltpu.VMEM((keys, rows), jnp.float32),
            pltpu.VMEM((keys, HEAD_SIZE), jnp.float32),
            pltpu.VMEM((keys, HEAD_SIZE), jnp.float32),
            dma((DOC_SHARDS, KEY_VALUE_HEADS, 2)),
            dma((DOC_SHARDS, KEY_VALUE_HEADS, 2)),
            dma((2, KEY_VALUE_HEADS)),
            dma((2, KEY_VALUE_HEADS)),
            dma((2, shards)),
            dma((shards,)),
            dma((2, shards)),
            dma((2, shards)),
            dma((2, shards)),
            dma((2, shards)),
            dma((2, 3, shards)),
            dma((3, shards)),
            dma((4, shards)),
            dma((4, shards)),
            dma,
        ],
        compiler_params=pltpu.CompilerParams(
            vmem_limit_bytes=50 * 1024 * 1024, collective_id=1, has_side_effects=True
        ),
    )(lengths, *operands)


def finish_kernel(q_ref, kv_ref, w_ref, q_out, kv_out, in_out, buf, sems):
    chunks = sems.shape[0] - 2
    step = buf.shape[1] // chunks
    qc = pltpu.make_async_copy(q_ref, q_out, sems.at[chunks])
    kc = pltpu.make_async_copy(kv_ref, kv_out, sems.at[chunks + 1])
    qc.start()
    kc.start()
    def cp(n):
        cols = pl.ds(n * step, step)
        return pltpu.make_async_copy(buf.at[:, cols], in_out.at[:, cols], sems.at[n])
    for n in range(chunks):
        buf[:, n * step:(n + 1) * step] = dot(kv_ref[...], w_ref[n * step:(n + 1) * step, :], ((1,), (1,))).astype(jnp.bfloat16)
        cp(n).start()
    for n in range(chunks):
        cp(n).wait()
    qc.wait()
    kc.wait()


def finish(grad_query, grad_kv, weight):
    rows, width = grad_query.shape
    feats = weight.shape[0]
    anyspec = pl.BlockSpec(memory_space=pl.ANY)
    vm = pl.BlockSpec(memory_space=pltpu.VMEM)
    return pl.pallas_call(
        finish_kernel,
        in_specs=[vm, vm, vm],
        out_specs=[anyspec] * 3,
        out_shape=[
            jax.ShapeDtypeStruct((rows, width), jnp.bfloat16),
            jax.ShapeDtypeStruct(grad_kv.shape, jnp.bfloat16),
            jax.ShapeDtypeStruct((rows, feats), jnp.bfloat16),
        ],
        scratch_shapes=[pltpu.VMEM((rows, feats), jnp.bfloat16), pltpu.SemaphoreType.DMA((10,))],
        compiler_params=pltpu.CompilerParams(vmem_limit_bytes=20*1024*1024),
    )(grad_query, grad_kv, weight)


def body(query, key_value_rows, grad_out, doc_lengths, key_value_weight):
    shape = (lax.axis_size("fsdp"), lax.axis_size("ctx"))
    run = plane_gradients if shape[0] == 4 and shape[1] == 8 else gradients
    grad_query, grad_kv, weight = run(
        shape, doc_lengths, query[0], grad_out[0], key_value_rows[0], key_value_weight
    )
    grad_query, grad_kv, grad_input = finish(grad_query, grad_kv, weight)
    return (grad_query[None], grad_kv[None], grad_input[None])


def solution(mesh):
    in_specs = (
        P("fsdp", "ctx", None),
        P("fsdp", "ctx", None),
        P("fsdp", "ctx", None),
        P("fsdp", None),
        P(("fsdp", "ctx"), None),
    )
    out_specs = (P("fsdp", "ctx", None), P("fsdp", "ctx", None), P("fsdp", "ctx", None))
    return jax.shard_map(body, mesh=mesh, in_specs=in_specs, out_specs=out_specs, check_vma=False)
```

```python
import functools

import jax
import jax.numpy as jnp
from jax import lax
from jax.experimental import pallas as pl
from jax.experimental.pallas import tpu as pltpu
from jax.sharding import PartitionSpec as P

QUERY_HEAD_COUNT = 32
KEY_VALUE_HEADS = 4
HEAD_SIZE = 128
DOC_SHARDS = 2
GROUP = QUERY_HEAD_COUNT // KEY_VALUE_HEADS
STEP = 2
LOG2E = 1.4426950408889634


def dot(a, b, dims):
    return lax.dot_general(a, b, (dims, ((), ())), preferred_element_type=jnp.float32)


def gradients_kernel(
    shape, lengths, query_hbm, grad_hbm, kv_hbm, w_own, grad_query, grad_kv, w_all,
    query, grad, kv0, in_sem, kv_sem,
    window, staged, landed, own, bias, dk, dv,
    kv_send, kv_recv, g_send, g_recv, z_send, r_send, l_send, p_send, w_recv, p_recv, local_sem,
):
    shards, count = shape
    chips = count // 2
    half = chips // 2
    width = int(chips ** 0.5)
    rows = query.shape[0]
    group_width = GROUP * HEAD_SIZE
    w_rows = w_own.shape[0]
    keys = (DOC_SHARDS + 1) * rows
    scale = HEAD_SIZE ** (-0.5)
    z = lax.axis_index("fsdp")
    me = lax.axis_index("ctx")
    core = lax.rem(me, 2)
    chip = me // 2
    line = chip // width
    column = lax.rem(chip, width)
    odd = lax.rem(line, 2)
    place = line * width + column + odd * (width - 1 - 2 * column)

    def ring_ctx(spot):
        spot = lax.rem(spot + chips, chips)
        row = spot // width
        col = lax.rem(spot, width)
        return 2 * (row * width + col + lax.rem(row, 2) * (width - 1 - 2 * col)) + core

    right = ring_ctx(place + 1)
    left = ring_ctx(place - 1)
    partner = me + 1 - 2 * core

    def query_in(g):
        cols = pl.ds(pl.multiple_of(g * group_width, HEAD_SIZE), group_width)
        return pltpu.make_async_copy(query_hbm.at[:, cols], query.at[:, cols], in_sem.at[0, g])

    def grad_in(g):
        cols = pl.ds(pl.multiple_of(g * group_width, HEAD_SIZE), group_width)
        return pltpu.make_async_copy(grad_hbm.at[:, cols], grad.at[:, cols], in_sem.at[1, g])

    kv_in = pltpu.make_async_copy(kv_hbm, kv0, kv_sem)
    kv_in.start()
    for g in range(KEY_VALUE_HEADS):
        query_in(g).start()
        grad_in(g).start()

    barrier = pltpu.get_barrier_semaphore()
    peers = [(z, lax.rem(me + o + count, count)) for o in (1, 2, -1, -2)]
    peers += [(lax.rem(z + r, shards), me) for r in range(1, shards)]
    peers += [(z, right), (z, left), (z, partner)]
    for peer in peers:
        pl.semaphore_signal(barrier, inc=1, device_id=peer, device_id_type=pl.DeviceIdType.MESH)
    pl.semaphore_wait(barrier, len(peers))

    def remote(src, dst, send, recv, device):
        return pltpu.make_async_remote_copy(
            src_ref=src, dst_ref=dst, send_sem=send, recv_sem=recv,
            device_id=device, device_id_type=pl.DeviceIdType.MESH,
        )

    def kv_copy(o, g, part):
        cols = pl.ds(pl.multiple_of((part * KEY_VALUE_HEADS + g) * HEAD_SIZE, HEAD_SIZE), HEAD_SIZE)
        return remote(
            kv_hbm.at[:, cols], window.at[o, :, cols], kv_send.at[o, g, part], kv_recv.at[o, g, part],
            (z, lax.rem(me + o + 1, count)),
        )

    def kv_relay(g, part):
        cols = pl.ds(pl.multiple_of((part * KEY_VALUE_HEADS + g) * HEAD_SIZE, HEAD_SIZE), HEAD_SIZE)
        return remote(
            window.at[1, :, cols], window.at[0, :, cols], kv_send.at[0, g, part], kv_recv.at[0, g, part],
            (z, partner),
        )

    sends_kv = [core == 0, me + 2 < count]
    relays_kv = (core == 1) & (me >= 2)

    def grad_copy(o, g):
        return remote(
            staged.at[o, g], landed.at[o, g], g_send.at[o, g], g_recv.at[o, g],
            (z, lax.rem(me - o - 1 + count, count)),
        )

    def block(zz, spot, flip=False):
        at = ring_ctx(spot)
        if flip:
            at = at + 1 - 2 * core
        return w_all.at[pl.ds(pl.multiple_of((zz * count + at) * w_rows, w_rows), w_rows)]

    def w_copy(zz, spot, sems, arrive, device, mine=False):
        spot = lax.rem(spot + chips, chips)
        src = w_own if mine else block(zz, spot)
        return remote(src, block(zz, spot), sems.at[zz, spot], arrive.at[zz, spot], device)

    def shard(r):
        return lax.rem(z - r + shards, shards)

    def w_arrived(r, t):
        w_copy(shard(r), place + t, r_send, w_recv, (z, right)).wait_recv()

    def takes_right(spot, zz):
        at = lax.rem(lax.rem(spot + chips, chips), 4)
        turn = lax.rem(zz, 4)
        even = lax.rem(at, 2) == 0
        return even | ((at == 1) & (turn >= 1)) | ((at == 3) & (turn >= 2))

    def each_copy(r, t, act):
        zz = shard(r)
        mine = r == 0 and t == 0
        if t == 0:
            act(w_copy(zz, place, r_send, w_recv, (z, right), mine))
            act(w_copy(zz, place, l_send, w_recv, (z, left), mine))
        elif -half + 1 <= t < 0:
            copy = w_copy(zz, place + t, r_send, w_recv, (z, right))
            if t > -half + 1:
                act(copy)
            else:
                pl.when(takes_right(place + 1, zz))(lambda: act(copy))
        elif 0 < t <= half - 1:
            copy = w_copy(zz, place + t, l_send, w_recv, (z, left))
            if t < half - 1:
                act(copy)
            else:
                pl.when(jnp.logical_not(takes_right(place - 1, zz)))(lambda: act(copy))
        act(w_copy(zz, place + t, p_send, p_recv, (z, partner), mine))

    def z_copy(r):
        to = lax.rem(z + r, shards)
        return remote(w_own, block(z, place), z_send.at[to], w_recv.at[z, place], (to, me))

    for g in range(KEY_VALUE_HEADS):
        for o in range(DOC_SHARDS):
            @pl.when(sends_kv[o])
            def _():
                kv_copy(o, g, 0).start()
                kv_copy(o, g, 1).start()

    for r in range(1, shards):
        z_copy(r).start()
    each_copy(0, 0, lambda c: c.start())
    local = pltpu.make_async_copy(w_own, block(z, place), local_sem)
    local.start()

    for o in range(DOC_SHARDS):
        @pl.when(me < o + 1)
        def _():
            window[o] = jnp.zeros(window.shape[1:], window.dtype)

        @pl.when(me + o + 1 >= count)
        def _():
            landed[o] = jnp.zeros(landed.shape[1:], landed.dtype)

    first = me * rows
    pos = first + lax.broadcasted_iota(jnp.int32, (1, rows), 1)
    start = jnp.zeros((1, rows), jnp.int32)
    end = jnp.int32(0)
    for d in range(lengths.shape[1]):
        end = end + lengths[0, d]
        start = jnp.where(pos >= end, end, start)
    key_pos = first - DOC_SHARDS * rows + lax.broadcasted_iota(jnp.int32, (keys, rows), 0)
    live = (key_pos >= start) & (key_pos <= pos)
    bias[...] = jnp.where(live, 0.0, -1e30)

    def group(g, carry):
        for o in reversed(range(DOC_SHARDS)):
            @pl.when(me >= o + 1)
            def _():
                kv_copy(o, g, 0).wait_recv()
                kv_copy(o, g, 1).wait_recv()

            if o == 1:
                @pl.when(relays_kv)
                def _():
                    kv_relay(g, 0).start()
                    kv_relay(g, 1).start()
        query_in(g).wait()
        grad_in(g).wait()

        @pl.when(g == 0)
        def _():
            kv_in.wait()
        kc = pl.ds(pl.multiple_of(g * HEAD_SIZE, HEAD_SIZE), HEAD_SIZE)
        vc = pl.ds(pl.multiple_of((g + KEY_VALUE_HEADS) * HEAD_SIZE, HEAD_SIZE), HEAD_SIZE)
        key = jnp.concatenate([window[1, :, kc], window[0, :, kc], kv0[:, kc]], axis=0)
        value = jnp.concatenate([window[1, :, vc], window[0, :, vc], kv0[:, vc]], axis=0)
        dk[...] = jnp.zeros_like(dk)
        dv[...] = jnp.zeros_like(dv)
        for h in range(GROUP):
            cols = pl.ds(pl.multiple_of((g * GROUP + h) * HEAD_SIZE, HEAD_SIZE), HEAD_SIZE)
            q = query[:, cols]
            go = grad[:, cols]
            s = dot(key, q, ((1,), (1,)))
            e = jnp.exp2(s * (scale * LOG2E) + bias[...])
            dp = dot(value, go, ((1,), (1,)))
            inv = 1.0 / jnp.sum(e, axis=0, keepdims=True)
            delta = jnp.sum(e * dp, axis=0, keepdims=True) * inv
            p = e * inv
            ds = (p * (dp - delta)).astype(jnp.bfloat16)
            dv[...] += dot(p.astype(jnp.bfloat16), go, ((1,), (0,)))
            dk[...] += dot(ds, q, ((1,), (0,)))
            dq = dot(key, ds, ((0,), (0,)))
            grad_query[:, cols] = (dq * scale).T.astype(jnp.bfloat16)
        for o in range(DOC_SHARDS):
            part = slice((DOC_SHARDS - 1 - o) * rows, (DOC_SHARDS - o) * rows)
            staged[o, g, 0] = (dk[part, :] * scale).astype(jnp.bfloat16)
            staged[o, g, 1] = dv[part, :].astype(jnp.bfloat16)
        own[g, 0] = dk[DOC_SHARDS * rows:, :] * scale
        own[g, 1] = dv[DOC_SHARDS * rows:, :]
        for o in range(DOC_SHARDS):
            @pl.when(me >= o + 1)
            def _():
                grad_copy(o, g).start()
        for k in range(KEY_VALUE_HEADS):
            turn = [r for r in range(1, shards) if min(r - 1, KEY_VALUE_HEADS - 1) == k]
            if turn:
                @pl.when(g == k)
                def _():
                    for r in turn:
                        w_arrived(r, 0)
                        each_copy(r, 0, lambda c: c.start())
        return carry

    lax.fori_loop(0, KEY_VALUE_HEADS, group, 0)

    for t in range(1, half):
        for r in range(shards):
            for side in (-t, t):
                w_arrived(r, side)
                each_copy(r, side, lambda c: c.start())

    for g in range(KEY_VALUE_HEADS):
        for o in range(DOC_SHARDS):
            @pl.when(me + o + 1 < count)
            def _():
                grad_copy(o, g).wait_recv()
        for part in range(2):
            total = own[g, part]
            for o in range(DOC_SHARDS):
                total = total + landed[o, g, part].astype(jnp.float32)
            at = (part * KEY_VALUE_HEADS + g) * HEAD_SIZE
            grad_kv[:, at:at + HEAD_SIZE] = total.astype(jnp.bfloat16)

    for r in range(shards):
        w_arrived(r, half)
        each_copy(r, half, lambda c: c.start())

    for r in range(shards):
        for t in range(-half + 1, half + 1):
            w_copy(shard(r), place + t, p_send, p_recv, (z, partner)).wait_recv()
            each_copy(r, t, lambda c: c.wait_send())
    for r in range(1, shards):
        z_copy(r).wait_send()
    local.wait()
    for g in range(KEY_VALUE_HEADS):
        @pl.when(relays_kv)
        def _():
            kv_relay(g, 0).wait_send()
            kv_relay(g, 1).wait_send()

        for o in range(DOC_SHARDS):
            @pl.when(sends_kv[o])
            def _():
                kv_copy(o, g, 0).wait_send()
                kv_copy(o, g, 1).wait_send()

            @pl.when(me >= o + 1)
            def _():
                grad_copy(o, g).wait_send()


def gradients(shape, lengths, query, grad, kv0, w_own):
    rows, width = query.shape
    keys = (DOC_SHARDS + 1) * rows
    w_rows, columns = w_own.shape
    shards, count = shape
    chips = count // 2
    vmem = pl.BlockSpec(memory_space=pltpu.VMEM)
    dma = pltpu.SemaphoreType.DMA
    parts = (DOC_SHARDS, KEY_VALUE_HEADS, 2, rows, HEAD_SIZE)
    return pl.pallas_call(
        functools.partial(gradients_kernel, shape),
        in_specs=[pl.BlockSpec(memory_space=pltpu.SMEM)] + [pl.BlockSpec(memory_space=pltpu.HBM)] * 4,
        out_specs=[pl.BlockSpec(memory_space=pltpu.VMEM)]*3,
        out_shape=[
            pltpu.VMEM((rows, width), jnp.bfloat16),
            pltpu.VMEM((rows, columns), jnp.bfloat16),
            pltpu.VMEM((w_rows * shards * count, columns), jnp.bfloat16),
        ],
        scratch_shapes=[
            pltpu.VMEM((rows, width), jnp.bfloat16),
            pltpu.VMEM((rows, width), jnp.bfloat16),
            pltpu.VMEM((rows, columns), jnp.bfloat16),
            dma((2, KEY_VALUE_HEADS)),
            dma,
            pltpu.VMEM((DOC_SHARDS, rows, columns), jnp.bfloat16),
            pltpu.VMEM(parts, jnp.bfloat16),
            pltpu.VMEM(parts, jnp.bfloat16),
            pltpu.VMEM(parts[1:], jnp.float32),
            pltpu.VMEM((keys, rows), jnp.float32),
            pltpu.VMEM((keys, HEAD_SIZE), jnp.float32),
            pltpu.VMEM((keys, HEAD_SIZE), jnp.float32),
            dma((DOC_SHARDS, KEY_VALUE_HEADS, 2)),
            dma((DOC_SHARDS, KEY_VALUE_HEADS, 2)),
            dma((DOC_SHARDS, KEY_VALUE_HEADS)),
            dma((DOC_SHARDS, KEY_VALUE_HEADS)),
            dma((shards,)),
            dma((shards, chips)),
            dma((shards, chips)),
            dma((shards, chips)),
            dma((shards, chips)),
            dma((shards, chips)),
            dma,
        ],
        compiler_params=pltpu.CompilerParams(
            vmem_limit_bytes=53*1024*1024, collective_id=0, has_side_effects=True
        ),
    )(lengths, query, grad, kv0, w_own)


def plan_of(shards):
    return {
        "start": (
            (("kv", 0), ("own", 0), ("kv", 1), ("kv", 2), ("kv", 3),),
            (("kv", 0), ("own", 0), ("kv", 1), ("kv", 2),),
        ),
        "early": (
            (("y", 0), ("line", 1), ("line", 2),),
            (("line", 1),),
        ),
        (0, 2): (
            (),
            (("y", 0), ("x", 0), ("kv", 3),),
        ),
        (0, 3): (
            (("x", 0),),
            (),
        ),
        (1, 1): (
            (("line", 3),),
            (),
        ),
        (1, 2): (
            (("bx", 2), ("by", 2),),
            (("line", 2),),
        ),
        (2, 0): (
            (("by", 1), ("x", 1),),
            (),
        ),
        (2, 1): (
            (("d", 0),),
            (("by", 1), ("x", 1), ("d", 0),),
        ),
        (2, 2): (
            (("y", 1), ("py", 1),),
            (("line", 3),),
        ),
        (2, 3): (
            (("bx", 1), ("px", 1),),
            (),
        ),
        (3, 0): (
            (("bd", 2), ("x", 2), ("px", 2), ("y", 2), ("py", 2), ("by", 3),),
            (),
        ),
        (3, 1): (
            (),
            (("x", 2), ("y", 1), ("py", 1),),
        ),
        (3, 2): (
            (("x", 3), ("y", 3), ("py", 3), ("bd", 1),),
            (),
        ),
        "after": (
            (("bx", 3), ("px", 3), ("bd", 3), ("d", 3), ("pd", 3), ("d", 1), ("pd", 1), ("d", 2), ("pd", 2),),
            (("by", 2), ("x", 3), ("y", 2), ("py", 2), ("y", 3), ("by", 3), ("py", 3), ("bx", 1), ("px", 1), ("d", 3), ("bx", 2), ("px", 2), ("bd", 1), ("bx", 3), ("px", 3), ("bd", 3), ("pd", 3), ("bd", 2), ("d", 2), ("pd", 2), ("d", 1), ("pd", 1),),
        ),
    }


def plane_kernel(
    shape, plan, lengths, query_hbm, grad_hbm, kv_hbm, w_own, grad_query, grad_kv, w_all,
    query, grad, kv0, in_sem, kv_sem,
    window, near, far, landed_near, landed_far, own, rest, bias, dk, dv,
    kv_send, kv_recv, g_send, g_recv, line_send, line_recv, side_send, side_recv,
    diag_send, diag_recv, tail_send, tail_recv, pair_send, pair_recv, local_sem,
):
    shards, count = shape
    chips = count // 2
    rows = query.shape[0]
    half = rows // 2
    group_width = GROUP * HEAD_SIZE
    w_rows = w_own.shape[0]
    part_one = w_rows * 56 // 128
    part_two = w_rows * 80 // 128
    keys = (DOC_SHARDS + 1) * rows
    scale = HEAD_SIZE ** (-0.5)
    z = lax.axis_index("fsdp")
    me = lax.axis_index("ctx")
    core = lax.rem(me, 2)
    chip = me // 2
    x = lax.rem(chip, 2)
    y = chip // 2
    even = x == y
    x_peer = me + 2 - 4 * x
    y_peer = me + 4 - 8 * y
    d_peer = x_peer + 4 - 8 * y
    sides = (x_peer, y_peer, d_peer)
    partner = me + 1 - 2 * core
    has_prev = chip >= 1
    has_next = chip < chips - 1
    up = lax.rem(z + 1, shards)
    down = lax.rem(z - 1 + shards, shards)

    def query_in(g):
        cols = pl.ds(pl.multiple_of(g * group_width, HEAD_SIZE), group_width)
        return pltpu.make_async_copy(query_hbm.at[:, cols], query.at[:, cols], in_sem.at[0, g])

    def grad_in(g):
        cols = pl.ds(pl.multiple_of(g * group_width, HEAD_SIZE), group_width)
        return pltpu.make_async_copy(grad_hbm.at[:, cols], grad.at[:, cols], in_sem.at[1, g])

    kv_in = pltpu.make_async_copy(kv_hbm, kv0, kv_sem)
    kv_in.start()
    for g in range(KEY_VALUE_HEADS):
        query_in(g).start()
        grad_in(g).start()

    barrier = pltpu.get_barrier_semaphore()
    peers = [(z, partner), (z, x_peer), (z, y_peer), (z, d_peer), (up, me), (down, me)]
    for peer in peers:
        pl.semaphore_signal(barrier, inc=1, device_id=peer, device_id_type=pl.DeviceIdType.MESH)
    pl.semaphore_wait(barrier, len(peers))

    def remote(src, dst, send, recv, device):
        return pltpu.make_async_remote_copy(
            src_ref=src, dst_ref=dst, send_sem=send, recv_sem=recv,
            device_id=device, device_id_type=pl.DeviceIdType.MESH,
        )

    def kv_cols(g, part):
        return pl.ds(pl.multiple_of((part * KEY_VALUE_HEADS + g) * HEAD_SIZE, HEAD_SIZE), HEAD_SIZE)

    def kv_far(g, part):
        cols = kv_cols(g, part)
        return remote(
            kv_hbm.at[:, cols], window.at[1, :, cols], kv_send.at[1, g, part], kv_recv.at[1, g, part],
            (z, lax.rem(me + 2, count)),
        )

    def kv_near(g, part):
        cols = kv_cols(g, part)
        return remote(
            kv_hbm.at[:, cols], window.at[0, :, cols], kv_send.at[0, g, part], kv_recv.at[0, g, part],
            (z, partner),
        )

    def kv_relay(g, part):
        cols = kv_cols(g, part)
        return remote(
            window.at[1, :, cols], window.at[0, :, cols], kv_send.at[0, g, part], kv_recv.at[0, g, part],
            (z, partner),
        )

    def near_copy(g):
        return remote(near.at[g], landed_near.at[g], g_send.at[0, g], g_recv.at[0, g], (z, partner))

    def far_copy(g):
        return remote(
            far.at[g], landed_far.at[g], g_send.at[1, g], g_recv.at[1, g],
            (z, lax.rem(me - 2 + count, count)),
        )

    def block(zz, c, first=0, last=None):
        size = (w_rows if last is None else last) - first
        return w_all.at[pl.ds(pl.multiple_of((zz * count + c) * w_rows + first, 8), size)]

    def line(zz, way, mine=False):
        device = (up if way == 0 else down, me)
        return remote(
            w_own if mine else block(zz, me), block(zz, me), line_send.at[way, zz], line_recv.at[zz], device
        )

    def side(k, zz, mine=False):
        last = w_rows if mine else part_two
        src = w_own if mine else block(zz, me, 0, last)
        return remote(
            src, block(zz, me, 0, last), side_send.at[k, zz], side_recv.at[k, zz], (z, sides[k])
        )

    def side_wait(k, zz, whole):
        last = w_rows if whole else part_two
        ref = block(zz, sides[k], 0, last)
        remote(ref, ref, side_send.at[k, zz], side_recv.at[k, zz], (z, sides[k])).wait_recv()

    def diag_two(zz, whole):
        ref = block(zz, x_peer, part_one, w_rows if whole else part_two)
        return remote(ref, ref, diag_send.at[1, zz], diag_recv.at[1, zz], (z, y_peer))

    def diag_one(zz, over_x):
        ref = block(zz, y_peer if over_x else x_peer, 0, part_one)
        device = (z, x_peer if over_x else y_peer)
        return remote(ref, ref, diag_send.at[0, zz], diag_recv.at[0, zz], device)

    def diag_wait(zz, whole):
        ref = block(zz, d_peer, 0, part_one)
        remote(ref, ref, diag_send.at[0, zz], diag_recv.at[0, zz], (z, y_peer)).wait_recv()
        ref = block(zz, d_peer, part_one, w_rows if whole else part_two)
        remote(ref, ref, diag_send.at[1, zz], diag_recv.at[1, zz], (z, y_peer)).wait_recv()

    def tail(k, zz, way):
        ref = block(zz, sides[k], part_two, w_rows)
        device = (up if way == 0 else down, me)
        return remote(ref, ref, tail_send.at[way, k, zz], tail_recv.at[k, zz], device)

    def pair(k, zz, mine=False):
        ref = block(zz, me if k == 3 else sides[k])
        return remote(
            w_own if mine else ref, ref, pair_send.at[k, zz], pair_recv.at[k, zz], (z, partner)
        )

    shorter = jnp.minimum(z, shards - 1 - z)
    longer = jnp.where(z < shards - 1 - z, 1, -1)

    def source(i):
        near_side = i <= 2 * shorter
        sign = jnp.where(near_side, 1 if i % 2 == 1 else -1, longer)
        distance = jnp.where(near_side, (i + 1) // 2, i - shorter)
        return z + sign * distance, sign

    def start(copy):
        copy.start()

    def finish(copy):
        copy.wait_send()

    def onward(make, sign, act):
        @pl.when((sign < 0) & (z < shards - 1))
        def _():
            act(make(0))

        @pl.when((sign > 0) & (z > 0))
        def _():
            act(make(1))

    def both_ways(make, act):
        @pl.when(z < shards - 1)
        def _():
            act(make(0))

        @pl.when(z > 0)
        def _():
            act(make(1))

    def own_line(act):
        both_ways(lambda way: line(z, way, True), act)

    def relay_x(zz, whole, act):
        act(diag_two(zz, whole))

        @pl.when(jnp.logical_not(even))
        def _():
            act(diag_one(zz, False))

    def relay_y(zz, act):
        @pl.when(even)
        def _():
            act(diag_one(zz, True))

    def event(kind, i, wait, act):
        if kind == "kv":
            @pl.when(has_next)
            def _():
                for part in range(2):
                    act(kv_far(i, part))
            return
        if kind == "own":
            own_line(act)
            act(side(1, z, True))
            act(side(0, z, True))
            return
        zz, sign = (z, 0) if i == 0 else source(i)
        if kind == "line":
            if wait:
                remote(block(zz, me), block(zz, me), line_send.at[0, zz], line_recv.at[zz], (up, me)).wait_recv()
            onward(lambda way: line(zz, way), sign, act)
            act(side(1, zz))
            act(side(0, zz))
            act(pair(3, zz))
        elif kind == "x":
            if wait:
                side_wait(0, zz, i == 0)
            relay_x(zz, i == 0, act)
            if i == 0:
                both_ways(lambda way: tail(0, zz, way), act)
                act(pair(0, zz))
        elif kind == "y":
            if wait:
                side_wait(1, zz, i == 0)
            relay_y(zz, act)
            if i == 0:
                both_ways(lambda way: tail(1, zz, way), act)
                act(pair(1, zz))
        elif kind == "d":
            if wait:
                diag_wait(zz, i == 0)
            if i == 0:
                both_ways(lambda way: tail(2, zz, way), act)
                act(pair(2, zz))
        elif kind in ("bx", "by", "bd"):
            k = ("bx", "by", "bd").index(kind)
            if wait:
                ref = block(zz, sides[k], part_two, w_rows)
                remote(ref, ref, tail_send.at[0, k, zz], tail_recv.at[k, zz], (up, me)).wait_recv()
            onward(lambda way: tail(k, zz, way), sign, act)
        elif kind in ("px", "py", "pd"):
            act(pair(("px", "py", "pd").index(kind), zz))

    at_end = (z == 0) | (z == shards - 1)

    def serve(key, now=True):
        for place, events in zip((jnp.logical_not(at_end), at_end), plan.get(key, ((), ()))):
            if events:
                @pl.when(place & now)
                def _():
                    for kind, i in events:
                        event(kind, i, True, start)

    def kv_forward(g):
        @pl.when(has_prev)
        def _():
            for part in range(2):
                kv_far(g, part).wait_recv()

        @pl.when(has_prev & (core == 1))
        def _():
            for part in range(2):
                kv_relay(g, part).start()

    serve("start")
    for g in range(KEY_VALUE_HEADS):
        @pl.when(core == 0)
        def _():
            for part in range(2):
                kv_near(g, part).start()
    pair(3, z, True).start()
    local = pltpu.make_async_copy(w_own, block(z, me), local_sem)
    local.start()

    @pl.when(me < 1)
    def _():
        window[0] = jnp.zeros(window.shape[1:], window.dtype)

    @pl.when(me < 2)
    def _():
        window[1] = jnp.zeros(window.shape[1:], window.dtype)

    first = me * rows
    pos = first + lax.broadcasted_iota(jnp.int32, (1, rows), 1)
    begin = jnp.zeros((1, rows), jnp.int32)
    end = jnp.int32(0)
    for d in range(lengths.shape[1]):
        end = end + lengths[0, d]
        begin = jnp.where(pos >= end, end, begin)
    key_pos = first - DOC_SHARDS * rows + lax.broadcasted_iota(jnp.int32, (keys, rows), 0)
    live = (key_pos >= begin) & (key_pos <= pos)
    bias[...] = jnp.where(live, 0.0, -1e30)

    def send_far(g):
        @pl.when(has_prev & (core == 1))
        def _():
            near_copy(g).wait_recv()
            for part in range(2):
                far[g, part] = (rest[part] + landed_near[g, part].astype(jnp.float32)).astype(jnp.bfloat16)

        @pl.when(has_prev & (core == 0))
        def _():
            for part in range(2):
                far[g, part] = rest[part].astype(jnp.bfloat16)

        @pl.when(has_prev)
        def _():
            far_copy(g).start()

    def blocks(a):
        return a[:half, :half], a[half:keys - half], a[keys - half:, half:]

    def joined(top, middle, bottom):
        empty = jnp.zeros((half, half), top.dtype)
        return jnp.concatenate(
            [jnp.concatenate([top, empty], axis=1), middle, jnp.concatenate([empty, bottom], axis=1)], axis=0
        )

    def column_sum(top, middle, bottom):
        total = jnp.sum(middle, axis=0, keepdims=True)
        return total + jnp.concatenate(
            [jnp.sum(top, axis=0, keepdims=True), jnp.sum(bottom, axis=0, keepdims=True)], axis=1
        )

    def split(row):
        return row[:, :half], row, row[:, half:]

    def heads(g, which, key, value):
        all_p, all_ds, all_q, all_go = [], [], [], []
        for h in which:
            cols = pl.ds(pl.multiple_of((g * GROUP + h) * HEAD_SIZE, HEAD_SIZE), HEAD_SIZE)
            q = query[:, cols]
            go = grad[:, cols]
            s = dot(key, q, ((1,), (1,)))
            dp = blocks(dot(value, go, ((1,), (1,))))
            b = (bias[:half, :half], bias[half:keys - half, :], bias[keys - half:, half:])
            e = [jnp.exp2(si * (scale * LOG2E) + bi) for si, bi in zip(blocks(s), b)]
            inv = 1.0 / column_sum(*e)
            delta = column_sum(*[ei * di for ei, di in zip(e, dp)]) * inv
            p = [ei * ii for ei, ii in zip(e, split(inv))]
            ds = [(pi * (di - li)).astype(jnp.bfloat16) for pi, di, li in zip(p, dp, split(delta))]
            all_p.append(joined(*[pi.astype(jnp.bfloat16) for pi in p]))
            all_ds.append(joined(*ds))
            all_q.append(q)
            all_go.append(go)
        p = jnp.concatenate(all_p, axis=1)
        ds = jnp.concatenate(all_ds, axis=1)
        return (
            dot(p, jnp.concatenate(all_go, axis=0), ((1,), (0,))),
            dot(ds, jnp.concatenate(all_q, axis=0), ((1,), (0,))),
            dot(key, ds, ((0,), (0,))),
        )

    def group(g, carry):
        @pl.when(me >= 1)
        def _():
            for part in range(2):
                kv_near(g, part).wait_recv()
        query_in(g).wait()
        grad_in(g).wait()

        kc = pl.ds(pl.multiple_of(g * HEAD_SIZE, HEAD_SIZE), HEAD_SIZE)
        vc = pl.ds(pl.multiple_of((g + KEY_VALUE_HEADS) * HEAD_SIZE, HEAD_SIZE), HEAD_SIZE)
        for n in range(0, GROUP, STEP):
            key = jnp.concatenate([window[1, :, kc], window[0, :, kc], kv0[:, kc]], axis=0)
            value = jnp.concatenate([window[1, :, vc], window[0, :, vc], kv0[:, vc]], axis=0)
            dv_part, dk_part, dq = heads(g, range(n, n + STEP), key, value)
            if n == 0:
                dv[...] = dv_part
                dk[...] = dk_part
            else:
                dv[...] += dv_part
                dk[...] += dk_part
            for j in range(STEP):
                cols = pl.ds(pl.multiple_of((g * GROUP + n + j) * HEAD_SIZE, HEAD_SIZE), HEAD_SIZE)
                grad_query[:, cols] = (dq[:, j * rows:(j + 1) * rows] * scale).T.astype(jnp.bfloat16)
            if n == 0:
                @pl.when(g >= 1)
                def _():
                    send_far(g - 1)
            if n == GROUP - STEP:
                @pl.when(g < KEY_VALUE_HEADS - 1)
                def _():
                    kv_forward(g + 1)
            for k in range(KEY_VALUE_HEADS):
                serve((k, n // STEP), g == k)
        near[g, 0] = (dk[rows:2 * rows, :] * scale).astype(jnp.bfloat16)
        near[g, 1] = dv[rows:2 * rows, :].astype(jnp.bfloat16)

        @pl.when(me >= 1)
        def _():
            near_copy(g).start()
        rest[0] = dk[:rows, :] * scale
        rest[1] = dv[:rows, :]
        own[g, 0] = dk[2 * rows:, :] * scale
        own[g, 1] = dv[2 * rows:, :]
        return carry

    serve("early")
    kv_forward(0)
    kv_in.wait()
    lax.fori_loop(0, KEY_VALUE_HEADS, group, 0)
    send_far(KEY_VALUE_HEADS - 1)
    serve("after")

    for g in range(KEY_VALUE_HEADS):
        @pl.when(core == 0)
        def _():
            near_copy(g).wait_recv()
            for part in range(2):
                own[g, part] += landed_near[g, part].astype(jnp.float32)

        @pl.when(has_next)
        def _():
            far_copy(g).wait_recv()
            for part in range(2):
                own[g, part] += landed_far[g, part].astype(jnp.float32)
        for part in range(2):
            at = (part * KEY_VALUE_HEADS + g) * HEAD_SIZE
            grad_kv[:, at:at + HEAD_SIZE] = own[g, part].astype(jnp.bfloat16)

    for k in range(4):
        for zz in range(shards):
            ref = block(zz, partner if k == 3 else sides[k] + 1 - 2 * core)
            remote(ref, ref, pair_send.at[k, zz], pair_recv.at[k, zz], (z, partner)).wait_recv()

    pair(3, z, True).wait_send()
    for events, _ in plan.values():
        for kind, i in events:
            event(kind, i, False, finish)
    local.wait()
    for g in range(KEY_VALUE_HEADS):
        for part in range(2):
            @pl.when(core == 0)
            def _():
                kv_near(g, part).wait_send()

            @pl.when(has_prev & (core == 1))
            def _():
                kv_relay(g, part).wait_send()

        @pl.when(me >= 1)
        def _():
            near_copy(g).wait_send()

        @pl.when(has_prev)
        def _():
            far_copy(g).wait_send()


def plane_gradients(shape, lengths, query, grad, kv0, w_own):
    rows, width = query.shape
    keys = (DOC_SHARDS + 1) * rows
    w_rows, columns = w_own.shape
    shards, count = shape
    dma = pltpu.SemaphoreType.DMA
    terms = (KEY_VALUE_HEADS, 2, rows, HEAD_SIZE)
    operands = [pltpu.with_memory_space_constraint(a, pltpu.HBM) for a in (query, grad, kv0, w_own)]
    return pl.pallas_call(
        functools.partial(plane_kernel, shape, plan_of(shards)),
        in_specs=[pl.BlockSpec(memory_space=pltpu.SMEM)] + [pl.BlockSpec(memory_space=pltpu.HBM)] * 4,
        out_specs=[pl.BlockSpec(memory_space=pltpu.VMEM)] * 3,
        out_shape=[
            pltpu.VMEM((rows, width), jnp.bfloat16),
            pltpu.VMEM((rows, columns), jnp.bfloat16),
            pltpu.VMEM((w_rows * shards * count, columns), jnp.bfloat16),
        ],
        scratch_shapes=[
            pltpu.VMEM((rows, width), jnp.bfloat16),
            pltpu.VMEM((rows, width), jnp.bfloat16),
            pltpu.VMEM((rows, columns), jnp.bfloat16),
            dma((2, KEY_VALUE_HEADS)),
            dma,
            pltpu.VMEM((DOC_SHARDS, rows, columns), jnp.bfloat16),
            pltpu.VMEM(terms, jnp.bfloat16),
            pltpu.VMEM(terms, jnp.bfloat16),
            pltpu.VMEM(terms, jnp.bfloat16),
            pltpu.VMEM(terms, jnp.bfloat16),
            pltpu.VMEM(terms, jnp.float32),
            pltpu.VMEM(terms[1:], jnp.float32),
            pltpu.VMEM((keys, rows), jnp.float32),
            pltpu.VMEM((keys, HEAD_SIZE), jnp.float32),
            pltpu.VMEM((keys, HEAD_SIZE), jnp.float32),
            dma((DOC_SHARDS, KEY_VALUE_HEADS, 2)),
            dma((DOC_SHARDS, KEY_VALUE_HEADS, 2)),
            dma((2, KEY_VALUE_HEADS)),
            dma((2, KEY_VALUE_HEADS)),
            dma((2, shards)),
            dma((shards,)),
            dma((2, shards)),
            dma((2, shards)),
            dma((2, shards)),
            dma((2, shards)),
            dma((2, 3, shards)),
            dma((3, shards)),
            dma((4, shards)),
            dma((4, shards)),
            dma,
        ],
        compiler_params=pltpu.CompilerParams(
            vmem_limit_bytes=50 * 1024 * 1024, collective_id=1, has_side_effects=True
        ),
    )(lengths, *operands)


def finish_kernel(q_ref, kv_ref, w_ref, q_out, kv_out, in_out, buf, sems):
    chunks = sems.shape[0] - 2
    step = buf.shape[1] // chunks
    qc = pltpu.make_async_copy(q_ref, q_out, sems.at[chunks])
    kc = pltpu.make_async_copy(kv_ref, kv_out, sems.at[chunks + 1])
    qc.start()
    kc.start()
    def cp(n):
        cols = pl.ds(n * step, step)
        return pltpu.make_async_copy(buf.at[:, cols], in_out.at[:, cols], sems.at[n])
    for n in range(chunks):
        buf[:, n * step:(n + 1) * step] = dot(kv_ref[...], w_ref[n * step:(n + 1) * step, :], ((1,), (1,))).astype(jnp.bfloat16)
        cp(n).start()
    for n in range(chunks):
        cp(n).wait()
    qc.wait()
    kc.wait()


def finish(grad_query, grad_kv, weight):
    rows, width = grad_query.shape
    feats = weight.shape[0]
    anyspec = pl.BlockSpec(memory_space=pl.ANY)
    vm = pl.BlockSpec(memory_space=pltpu.VMEM)
    return pl.pallas_call(
        finish_kernel,
        in_specs=[vm, vm, vm],
        out_specs=[anyspec] * 3,
        out_shape=[
            jax.ShapeDtypeStruct((rows, width), jnp.bfloat16),
            jax.ShapeDtypeStruct(grad_kv.shape, jnp.bfloat16),
            jax.ShapeDtypeStruct((rows, feats), jnp.bfloat16),
        ],
        scratch_shapes=[pltpu.VMEM((rows, feats), jnp.bfloat16), pltpu.SemaphoreType.DMA((10,))],
        compiler_params=pltpu.CompilerParams(vmem_limit_bytes=20*1024*1024),
    )(grad_query, grad_kv, weight)


def body(query, key_value_rows, grad_out, doc_lengths, key_value_weight):
    shape = (lax.axis_size("fsdp"), lax.axis_size("ctx"))
    run = plane_gradients if shape[0] == 4 and shape[1] == 8 else gradients
    grad_query, grad_kv, weight = run(
        shape, doc_lengths, query[0], grad_out[0], key_value_rows[0], key_value_weight
    )
    grad_query, grad_kv, grad_input = finish(grad_query, grad_kv, weight)
    return (grad_query[None], grad_kv[None], grad_input[None])


def solution(mesh):
    in_specs = (
        P("fsdp", "ctx", None),
        P("fsdp", "ctx", None),
        P("fsdp", "ctx", None),
        P("fsdp", None),
        P(("fsdp", "ctx"), None),
    )
    out_specs = (P("fsdp", "ctx", None), P("fsdp", "ctx", None), P("fsdp", "ctx", None))
    return jax.shard_map(body, mesh=mesh, in_specs=in_specs, out_specs=out_specs, check_vma=False)
```
